256 devices in a mesh: gx: 16 (over x, y), gy: 16 (over z, core).
Axes of the slice: x: 4, y: 4, z: 8, core: 2. Of those that a mesh axis runs over, the one named last changes fastest.
Arguments:
- raw_basis: float32 [512, 256, 4, 128], P('gx', 'gy'), may hold values from -600 to 600, as said below
- coefficients: float32 [4, 512, 256, 4], P(None, 'gx', 'gy'), may hold values from 0.25 to 4
- nominal_weights: float32 [4], replicated, may hold values from 0.5 to 2
Outputs:
- ortho_basis: float32 [512, 256, 4, 128], P('gx', 'gy')
- nominal_image: float32 [512, 256, 4, 128], P('gx', 'gy')
- reduced_ops: float32 [4, 128, 128], replicated
- residual_grams: float32 [10, 128, 128], replicated
The draws below stay inside these ranges and needn't reach their ends.
Inputs may be any that keep to these rules, and one draw needn't show every extreme that they name: `raw_basis`: the columns are linearly independent.
All inputs are finite; a program needn't handle non-finite values.
Results may differ from the reference program's by a relative error of at most 0.0001.
Values sent between devices are 32-bit elements; how exact they have to be, the bound alone decides.
No kernel may reach another device: no remote copies, remote signals or barrier semaphores. Data moves between devices by JAX's collectives and lax.ppermute only.
A program may use at most 64 MiB of HBM per device.

```python
import math
import jax
import jax.numpy as jnp
from jax import lax

R = 128
TERMS = 4
NZ = 4
NX = 512
NY = 256


def draw_raw_basis(key, part):
    subkeys = jax.random.split(jax.random.fold_in(key, 17), 3)
    extent = (NX, NY, NZ, R)
    noise = jnp.clip(jax.random.normal(subkeys[0], extent, jnp.float32), -6.0, 6.0)
    scales = jnp.exp(jax.random.uniform(subkeys[1], (R,), jnp.float32, 0.0, math.log(10.0)))
    mixing = jnp.eye(R, dtype=jnp.float32) + jnp.triu(jax.random.normal(subkeys[2], (R, R), jnp.float32), 1) * (0.5 / math.sqrt(R))
    mixing = scales[:, None] * mixing
    mixed = jnp.dot(noise.reshape(-1, R), mixing, precision=lax.Precision.HIGHEST).reshape(extent)
    return jnp.clip(mixed, -600.0, 600.0)


def steps_of(own_key, shape, shards, least, top_value):
    loudness, own = 1.0, jax.random.fold_in(own_key, 6)
    for dim, shards_of in shards:
        heights = jnp.exp(jax.random.uniform(jax.random.fold_in(own, dim), (shards_of,), jnp.float32, least / len(shards), top_value / len(shards)))
        loudness = loudness * jnp.repeat(heights, shape[dim] // shards_of).reshape([-1 if axis == dim else 1 for axis in range(len(shape))])
    return loudness


def setup_inputs(seed: int = 0) -> dict:
    keys = jax.random.split(jax.random.key(seed), 4)
    return {
        "raw_basis": draw_raw_basis(jax.random.fold_in(keys[3], 71), 0),
        "coefficients": jnp.clip(jnp.exp(math.log(4.0) - 2.7725887 * jax.random.uniform(keys[1], (TERMS, NX, NY, NZ), jnp.float32) ** steps_of(keys[1], (TERMS, NX, NY, NZ), ((1, 16), (2, 16)), -0.2, 0.2)), 0.25, 4.0),
        "nominal_weights": jnp.clip(jnp.exp(jax.random.uniform(keys[2], (TERMS,), jnp.float32, math.log(0.5), math.log(2.0))), 0.5, 2.0),
    }


directions = ((1, 0, 0), (-1, 0, 0), (0, 1, 0), (0, -1, 0), (0, 0, 1), (0, 0, -1))
operator_pairs = ((0, 0), (0, 1), (0, 2), (0, 3), (1, 1), (1, 2), (1, 3), (2, 2), (2, 3), (3, 3))

def window(values, leading, along_x, along_y, along_z):
    selector = [slice(None)] * values.ndim
    for position, offset in zip(range(leading, leading + 3), (along_x, along_y, along_z)):
        selector[position] = slice(1 + offset, values.shape[position] - 1 + offset)
    return values[tuple(selector)]

def apply_all(padded_basis, padded_coef):
    centre = window(padded_basis, 0, 0, 0, 0)
    centre_coef = window(padded_coef, 1, 0, 0, 0)
    images = [jnp.zeros_like(centre) for member in range(4)]
    for direction in directions:
        differ = centre - window(padded_basis, 0, *direction)
        weights = 0.5 * (centre_coef + window(padded_coef, 1, *direction))
        images = [images[member] + weights[member][..., None] * differ for member in range(4)]
    return jnp.stack(images)

def weighted(nominal_weights, images):
    total = nominal_weights[0] * images[0]
    for member in range(1, 4):
        total = total + nominal_weights[member] * images[member]
    return total

def inverse_factor(gram):
    factor = jnp.linalg.cholesky(gram)
    return jax.scipy.linalg.solve_triangular(factor, jnp.eye(gram.shape[0], dtype=gram.dtype), lower=True)

def reference(raw_basis, coefficients, nominal_weights):
    total_cells = NX * NY * NZ
    flat = raw_basis.reshape(-1, R)
    gram = jnp.einsum('cr,cs->rs', flat, flat, precision=lax.Precision.HIGHEST) / total_cells
    inverse = inverse_factor(gram)
    ortho_flat = jnp.dot(flat, inverse.T, precision=lax.Precision.HIGHEST)
    ortho_basis = ortho_flat.reshape(raw_basis.shape)
    padded_basis = jnp.pad(ortho_basis, ((1, 1), (1, 1), (1, 1), (0, 0)))
    padded_coef = jnp.pad(coefficients, ((0, 0), (1, 1), (1, 1), (1, 1)))
    images = apply_all(padded_basis, padded_coef)
    nominal_image = weighted(nominal_weights, images)
    image_flat = images.reshape(4, -1, R)
    reduced_ops = jnp.einsum('cr,kcs->krs', ortho_flat, image_flat, precision=lax.Precision.HIGHEST) / total_cells
    residual_grams = jnp.stack([jnp.einsum('cr,cs->rs', image_flat[first_op], image_flat[second_op], precision=lax.Precision.HIGHEST) for first_op, second_op in operator_pairs]) / total_cells
    return (ortho_basis, nominal_image, reduced_ops, residual_grams)
```

```python
import jax
import jax.numpy as jnp
from jax import lax
from jax.experimental import pallas as pl
from jax.experimental.pallas import tpu as pltpu
from jax.sharding import PartitionSpec as P

R = 128
TERMS = 4
operator_pairs = ((0, 0), (0, 1), (0, 2), (0, 3), (1, 1), (1, 2), (1, 3), (2, 2), (2, 3), (3, 3))
crossed_pairs = tuple(pair for pair in operator_pairs if pair[0] != pair[1])
HIGHEST = lax.Precision.HIGHEST
f32, bf16 = jnp.float32, jnp.bfloat16

SLOTS = 12
HALF = SLOTS // 2 * R
SLAB = 64
CHUNK = 4


def faces_kernel(basis, coef, x_low, x_high, y_low, y_high):
    lane = lax.broadcasted_iota(jnp.int32, (SLAB, R), 1)
    slabs = basis.shape[0] // SLAB
    x_low[0:SLAB, :] = basis[0:SLAB, :]
    x_high[0:SLAB, :] = basis[(slabs - 1) * SLAB : slabs * SLAB, :]
    low = jnp.zeros((SLAB, R), f32)
    high = jnp.zeros((SLAB, R), f32)
    for k in range(TERMS):
        rows = coef[k * SLAB : (k + 1) * SLAB, :]
        low = jnp.where(lane == k, rows[:, 0:1], low)
        high = jnp.where(lane == k, rows[:, slabs - 1 : slabs], high)
    x_low[SLAB : 2 * SLAB, :] = low
    x_high[SLAB : 2 * SLAB, :] = high
    for x in range(slabs):
        y_low[4 * x : 4 * x + 4, :] = basis[x * SLAB : x * SLAB + 4, :]
        y_high[4 * x : 4 * x + 4, :] = basis[x * SLAB + SLAB - 4 : (x + 1) * SLAB, :]
    y_low[4 * slabs :, :] = jnp.zeros((16, R), f32)
    y_high[4 * slabs :, :] = jnp.zeros((16, R), f32)
    for k in range(TERMS):
        y_low[4 * (slabs + k) : 4 * (slabs + k) + 4, 0:slabs] = coef[k * SLAB : k * SLAB + 4, :]
        y_high[4 * (slabs + k) : 4 * (slabs + k) + 4, 0:slabs] = coef[(k + 1) * SLAB - 4 : (k + 1) * SLAB, :]


def images_kernel(
    me, weights, basis, coef, from_left, from_right, from_below, from_above, mine, other, nominal,
    extended, face, top, bottom, product, packed,
):
    slabs = basis.shape[0] // SLAB
    extended[0:SLAB, :] = from_left[0:SLAB, :]
    extended[SLAB : (slabs + 1) * SLAB, :] = basis[...]
    extended[(slabs + 1) * SLAB :, :] = from_right[0:SLAB, :]
    product[...] = jnp.zeros_like(product)

    row = lax.broadcasted_iota(jnp.int32, (SLAB, R), 0)
    lane = lax.broadcasted_iota(jnp.int32, (SLAB, R), 1)
    level = row % 4
    row8 = lax.broadcasted_iota(jnp.int32, (8, R), 0)

    for k in range(TERMS):
        own = jnp.concatenate([coef[k * SLAB : (k + 1) * SLAB, :], jnp.zeros((SLAB, R - slabs), f32)], axis=1)
        right = jnp.where(lane == slabs, from_right[SLAB : 2 * SLAB, k : k + 1], own)
        left = jnp.where(lane == 0, from_left[SLAB : 2 * SLAB, k : k + 1], pltpu.roll(own, 1, 1))
        face[k, 0] = 0.5 * (left + right)
        pair = 4 * slabs + 8 * (k // 2)
        above = from_above[pair : pair + 8, :]
        below = from_below[pair : pair + 8, :]
        if k % 2 == 0:
            above = pltpu.roll(above, 4, 0)
        else:
            below = pltpu.roll(below, 4, 0)
        up = pltpu.roll(own, SLAB - 4, 0)
        up = jnp.concatenate([up[: SLAB - 8], jnp.where(row8 >= 4, above, up[SLAB - 8 :])], axis=0)
        down = pltpu.roll(own, 4, 0)
        down = jnp.concatenate([jnp.where(row8 < 4, below, down[:8]), down[8:]], axis=0)
        face[k, 1] = 0.5 * (own + up)
        face[k, 2] = 0.5 * (own + down)
        face[k, 3] = 0.5 * (own + jnp.where(level < 3, pltpu.roll(own, SLAB - 1, 0), 0.0))
        face[k, 4] = 0.5 * (own + jnp.where(level > 0, pltpu.roll(own, 1, 0), 0.0))

    def chunk(c, carry):
        shift = lax.rem(R - c * CHUNK, R)
        moved = [[pltpu.roll(face[k, f], shift, 1) for f in range(5)] for k in range(TERMS)]
        for s in range(CHUNK):
            x = c * CHUNK + s
            base = pl.multiple_of(x * SLAB, SLAB)
            v = extended[pl.ds(pl.multiple_of(base + SLAB, SLAB), SLAB), :]
            pair = pl.multiple_of((c * (CHUNK // 2) + s // 2) * 8, 8)
            above = from_above[pl.ds(pair, 8), :]
            below = from_below[pl.ds(pair, 8), :]
            if s % 2 == 0:
                above = pltpu.roll(above, 4, 0)
            else:
                below = pltpu.roll(below, 4, 0)
            up = pltpu.roll(v, SLAB - 4, 0)
            up = jnp.concatenate([up[: SLAB - 8], jnp.where(row8 >= 4, above, up[SLAB - 8 :])], axis=0)
            down = pltpu.roll(v, 4, 0)
            down = jnp.concatenate([jnp.where(row8 < 4, below, down[:8]), down[8:]], axis=0)
            steps = (
                v - extended[pl.ds(base, SLAB), :],
                v - extended[pl.ds(pl.multiple_of(base + 2 * SLAB, SLAB), SLAB), :],
                v - up,
                v - down,
                v - jnp.where(level < 3, pltpu.roll(v, SLAB - 1, 0), 0.0),
                v - jnp.where(level > 0, pltpu.roll(v, 1, 0), 0.0),
            )
            total = jnp.zeros((SLAB, R), f32)
            for block in range(TERMS + 1):
                if block == 0:
                    value = v
                else:
                    k = block - 1
                    columns = [moved[k][0][:, s : s + 1], moved[k][0][:, s + 1 : s + 2]]
                    columns += [moved[k][f][:, s : s + 1] for f in range(1, 5)]
                    value = columns[0] * steps[0]
                    for column, step in zip(columns[1:], steps[1:]):
                        value = value + column * step
                    total = total + weights[k] * value
                high = value.astype(bf16)
                low = (value - high.astype(f32)).astype(bf16)
                top[s * SLAB : (s + 1) * SLAB, block * R : (block + 1) * R] = high
                bottom[s * SLAB : (s + 1) * SLAB, block * R : (block + 1) * R] = low
            nominal[pl.ds(base, SLAB), :] = total
        turned = top[...].T
        width = (TERMS + 1) * R
        for start in range(0, 2 * width, 256):
            rows = min(start + 256, width)
            if start + 256 <= width:
                right = top[:, start : start + 256]
            elif start < width:
                right = jnp.concatenate([top[:, start:width], bottom[:, 0 : start + 256 - width]], axis=1)
            else:
                right = bottom[:, start - width : start + 256 - width]
            product[0:rows, start : start + 256] += jnp.dot(turned[0:rows], right, preferred_element_type=f32)
        return carry

    lax.fori_loop(0, slabs // CHUNK, chunk, 0)

    width = (TERMS + 1) * R

    def gram(a, b):
        high = product[a * R : (a + 1) * R, b * R : (b + 1) * R]
        first = product[a * R : (a + 1) * R, width + b * R : width + (b + 1) * R]
        second = product[b * R : (b + 1) * R, width + a * R : width + (a + 1) * R]
        return high + first + second.T

    r = lax.broadcasted_iota(jnp.int32, (R, R), 0)
    c = lax.broadcasted_iota(jnp.int32, (R, R), 1)
    packed[0:R, :] = gram(0, 0)
    symmetric = [(0, k + 1) for k in range(TERMS)] + [(k + 1, k + 1) for k in range(TERMS)]
    packed[(SLOTS - 1) * R :, :] = jnp.zeros((R, R), f32)
    for p in range(4):
        one, two = gram(*symmetric[2 * p]), gram(*symmetric[2 * p + 1])
        packed[(p + 1) * R : (p + 2) * R, :] = jnp.where(c >= r, one, two)
        packed[(SLOTS - 1) * R + p : (SLOTS - 1) * R + p + 1, :] = jnp.sum(
            jnp.where(c == r, two, 0.0), axis=0, keepdims=True
        )
    for q, (a, b) in enumerate(crossed_pairs):
        packed[(q + 5) * R : (q + 6) * R, :] = gram(a + 1, b + 1)
    mine[...] = packed[pl.ds(pl.multiple_of(me[0] * HALF, R), HALF), :]
    other[...] = packed[pl.ds(pl.multiple_of((1 - me[0]) * HALF, R), HALF), :]


def finish_kernel(me, mine, other, basis, nominal, ortho_out, nominal_out, reduced_out, residual_out, packed, inverse, *, cells):
    packed[pl.ds(pl.multiple_of(me[0] * HALF, R), HALF), :] = mine[...]
    packed[pl.ds(pl.multiple_of((1 - me[0]) * HALF, R), HALF), :] = other[...]
    scale = 1.0 / cells
    row8 = lax.broadcasted_iota(jnp.int32, (8, R), 0)
    lane8 = lax.broadcasted_iota(jnp.int32, (8, R), 1)
    blocks = R // 8
    left = [packed[8 * i : 8 * i + 8, :] * scale for i in range(blocks)]
    right = [jnp.where(row8 + 8 * i == lane8, 1.0, 0.0).astype(f32) for i in range(blocks)]
    for j in range(R):
        i0, r0 = divmod(j, 8)
        pivot_row = left[i0][r0 : r0 + 1, :]
        right_row = right[i0][r0 : r0 + 1, :]
        pivot = pivot_row[:, j : j + 1]
        inverse[j : j + 1, :] = right_row * (1.0 / jnp.sqrt(pivot))
        scaled_left = pivot_row * (1.0 / pivot)
        scaled_right = right_row * (1.0 / pivot)
        for i in range(i0, blocks):
            column = left[i][:, j : j + 1]
            if i == i0:
                if r0 == 7:
                    continue
                column = jnp.where(row8 > r0, column, 0.0)
            left[i] = left[i] - column * scaled_left
            right[i] = right[i] - column * scaled_right
    inv = inverse[...]
    inv_t = inv.T
    ortho_out[...] = jnp.dot(basis[...], inv_t, precision=HIGHEST, preferred_element_type=f32)
    nominal_out[...] = jnp.dot(nominal[...], inv_t, precision=HIGHEST, preferred_element_type=f32)

    r = lax.broadcasted_iota(jnp.int32, (R, R), 0)
    c = lax.broadcasted_iota(jnp.int32, (R, R), 1)

    def moved(matrix):
        half = jnp.dot(matrix * scale, inv_t, precision=HIGHEST, preferred_element_type=f32)
        return jnp.dot(inv, half, precision=HIGHEST, preferred_element_type=f32)

    for p in range(4):
        pair = packed[(p + 1) * R : (p + 2) * R, :]
        turned = pair.T
        diagonal = packed[(SLOTS - 1) * R + p : (SLOTS - 1) * R + p + 1, :]
        one = moved(jnp.where(c >= r, pair, turned))
        two = moved(jnp.where(c < r, pair, jnp.where(c == r, diagonal, turned)))
        if p < 2:
            reduced_out[2 * p] = one
            reduced_out[2 * p + 1] = two
        else:
            k = 2 * (p - 2)
            residual_out[operator_pairs.index((k, k))] = one
            residual_out[operator_pairs.index((k + 1, k + 1))] = two
    for q, (a, b) in enumerate(crossed_pairs):
        residual_out[operator_pairs.index((a, b))] = moved(packed[(q + 5) * R : (q + 6) * R, :])


def summed(values, half, groups):
    count = lax.axis_size("gx")
    width = values.shape[1]
    parts = values.reshape(count, -1, width)
    shard = jnp.sum(lax.all_to_all(parts, "gx", 0, 0), axis=0)
    depth = len(groups[0])
    along = jnp.broadcast_to(shard[None], (depth,) + shard.shape)
    shard = jnp.sum(lax.all_to_all(along, "gy", 0, 0, axis_index_groups=groups), axis=0)
    spread = jnp.broadcast_to(shard[None], (count,) + shard.shape)
    return lax.all_to_all(spread, "gx", 0, 0).reshape(values.shape)


def shards(raw_basis, coefficients, nominal_weights):
    nx, ny, nz, width = raw_basis.shape
    count_x, count_y = lax.axis_size("gx"), lax.axis_size("gy")
    cells = nx * ny * nz * count_x * count_y
    flat = raw_basis.reshape(-1, width)
    coef = jnp.transpose(coefficients, (0, 2, 3, 1)).reshape(-1, nx)
    vmem = pl.BlockSpec(memory_space=pltpu.VMEM)
    smem = pl.BlockSpec(memory_space=pltpu.SMEM)

    def array(*shape):
        return jax.ShapeDtypeStruct(shape, f32)

    y_rows = 4 * nx + 4 * TERMS
    x_low, x_high, y_low, y_high = pl.pallas_call(
        faces_kernel,
        out_shape=(array(2 * SLAB, R), array(2 * SLAB, R), array(y_rows, R), array(y_rows, R)),
        in_specs=[vmem, vmem],
        out_specs=(vmem,) * 4,
        name="faces",
    )(flat, coef)
    up_x = [(i, i + 1) for i in range(count_x - 1)]
    up_y = [(i, i + 1) for i in range(count_y - 1)]
    from_left = lax.ppermute(x_high, "gx", up_x)
    from_right = lax.ppermute(x_low, "gx", [(b, a) for a, b in up_x])
    from_below = lax.ppermute(y_high, "gy", up_y)
    from_above = lax.ppermute(y_low, "gy", [(b, a) for a, b in up_y])

    me = (lax.axis_index("gy") % 2).astype(jnp.int32).reshape(1)
    mine, other, raw_nominal = pl.pallas_call(
        images_kernel,
        out_shape=(array(HALF, R), array(HALF, R), array(nx * SLAB, R)),
        in_specs=[smem, smem] + [vmem] * 6,
        out_specs=(vmem,) * 3,
        scratch_shapes=[
            pltpu.VMEM(((nx + 2) * SLAB, R), f32),
            pltpu.VMEM((TERMS, 5, SLAB, R), f32),
            pltpu.VMEM((CHUNK * SLAB, (TERMS + 1) * R), bf16),
            pltpu.VMEM((CHUNK * SLAB, (TERMS + 1) * R), bf16),
            pltpu.VMEM(((TERMS + 1) * R, 2 * (TERMS + 1) * R), f32),
            pltpu.VMEM((SLOTS * R, R), f32),
        ],
        name="images",
    )(me, nominal_weights, flat, coef, from_left, from_right, from_below, from_above)

    swap = [(i, i ^ 1) for i in range(count_y)]
    groups = [list(range(core, count_y, 2)) for core in range(2)]
    mine = mine + lax.ppermute(other, "gy", swap)
    mine = summed(mine, HALF, groups)
    other = lax.ppermute(mine, "gy", swap)

    def finish(*refs):
        finish_kernel(*refs, cells=cells)

    ortho, nominal, reduced_ops, residual_grams = pl.pallas_call(
        finish,
        out_shape=(array(nx * SLAB, R), array(nx * SLAB, R), array(TERMS, R, R), array(len(operator_pairs), R, R)),
        in_specs=[smem] + [vmem] * 4,
        out_specs=(vmem,) * 4,
        scratch_shapes=[pltpu.VMEM((SLOTS * R, R), f32), pltpu.VMEM((R, R), f32)],
        name="finish",
    )(me, mine, other, flat, raw_nominal)
    shape = raw_basis.shape
    return (ortho.reshape(shape), nominal.reshape(shape), reduced_ops, residual_grams)


def solution(mesh):
    in_specs = (P("gx", "gy", None, None), P(None, "gx", "gy", None), P())
    out_specs = (P("gx", "gy", None, None), P("gx", "gy", None, None), P(), P())
    return jax.shard_map(shards, mesh=mesh, in_specs=in_specs, out_specs=out_specs, check_vma=False)
```

```python
import jax
import jax.numpy as jnp
from jax import lax
from jax.experimental import pallas as pl
from jax.experimental.pallas import tpu as pltpu
from jax.sharding import PartitionSpec as P

R = 128
TERMS = 4
operator_pairs = ((0, 0), (0, 1), (0, 2), (0, 3), (1, 1), (1, 2), (1, 3), (2, 2), (2, 3), (3, 3))
crossed_pairs = tuple(pair for pair in operator_pairs if pair[0] != pair[1])
HIGHEST = lax.Precision.HIGHEST
f32, bf16 = jnp.float32, jnp.bfloat16

HALF_SLOTS = 6
HALF = HALF_SLOTS * R
SLAB = 64
WIDTH = (TERMS + 1) * R
BLOCK = 32
halves = (
    ([(0, k + 1) for k in range(TERMS)], [(a + 1, b + 1) for a, b in crossed_pairs[:3]]),
    ([(k + 1, k + 1) for k in range(TERMS)], [(a + 1, b + 1) for a, b in crossed_pairs[3:]]),
)

def faces_kernel(basis, coef, x_low, x_high, y_low, y_high):
    lane = lax.broadcasted_iota(jnp.int32, (SLAB, R), 1)
    slabs = basis.shape[0] // SLAB
    x_low[0:SLAB, :] = basis[0:SLAB, :]
    x_high[0:SLAB, :] = basis[(slabs - 1) * SLAB : slabs * SLAB, :]
    low = jnp.zeros((SLAB, R), f32)
    high = jnp.zeros((SLAB, R), f32)
    for k in range(TERMS):
        rows = coef[k * SLAB : (k + 1) * SLAB, :]
        low = jnp.where(lane == k, rows[:, 0:1], low)
        high = jnp.where(lane == k, rows[:, slabs - 1 : slabs], high)
    x_low[SLAB : 2 * SLAB, :] = low
    x_high[SLAB : 2 * SLAB, :] = high
    for x in range(slabs):
        y_low[4 * x : 4 * x + 4, :] = basis[x * SLAB : x * SLAB + 4, :]
        y_high[4 * x : 4 * x + 4, :] = basis[x * SLAB + SLAB - 4 : (x + 1) * SLAB, :]
    y_low[4 * slabs :, :] = jnp.zeros((16, R), f32)
    y_high[4 * slabs :, :] = jnp.zeros((16, R), f32)
    for k in range(TERMS):
        y_low[4 * (slabs + k) : 4 * (slabs + k) + 4, 0:slabs] = coef[k * SLAB : k * SLAB + 4, :]
        y_high[4 * (slabs + k) : 4 * (slabs + k) + 4, 0:slabs] = coef[(k + 1) * SLAB - 4 : (k + 1) * SLAB, :]


def images_kernel(
    me, nominal_weights, basis, coef, from_left, from_right, from_below, from_above, mine, other, nominal,
    turned, above, below, face, top, bottom, product, squares, total,
):
    slabs = basis.shape[0] // SLAB
    groups = slabs // 2

    def slab(x):
        return basis[x * SLAB : (x + 1) * SLAB, :]

    for j in range(groups):
        turned[j + 1] = jnp.concatenate([slab(j), slab(j + groups)], axis=0).T
    turned[0] = jnp.concatenate([from_left[0:SLAB, :], slab(groups - 1)], axis=0).T
    turned[groups + 1] = jnp.concatenate([slab(groups), from_right[0:SLAB, :]], axis=0).T
    above[...] = from_above[0 : 4 * slabs, :].T
    below[...] = from_below[0 : 4 * slabs, :].T

    spot = lax.broadcasted_iota(jnp.int32, (groups, R), 1) % SLAB
    first = lax.broadcasted_iota(jnp.int32, (groups, R), 1) < SLAB
    group = lax.broadcasted_iota(jnp.int32, (groups, R), 0)
    level = spot % 4

    def joined(rows):
        return jnp.where(first, rows[0:groups], pltpu.roll(rows[groups:slabs], SLAB, 1))

    def flipped(tile):
        return jnp.concatenate([tile, jnp.zeros((R - tile.shape[0], R), f32)], axis=0).T

    left_coef = flipped(from_left[SLAB : 2 * SLAB, :])
    right_coef = flipped(from_right[SLAB : 2 * SLAB, :])
    above_coef = flipped(from_above[4 * slabs :, :])
    below_coef = flipped(from_below[4 * slabs :, :])
    for k in range(TERMS):
        rows = jnp.concatenate([coef[k * SLAB : (k + 1) * SLAB, :], jnp.zeros((SLAB, R - slabs), f32)], axis=1)
        own = joined(flipped(rows))
        half = pltpu.roll(own, SLAB, 1)
        left = jnp.where(first, left_coef[k : k + 1, :], half[groups - 1 : groups, :])
        left = jnp.where(group == 0, left, pltpu.roll(own, 1, 0))
        right = jnp.where(first, half[0:1, :], pltpu.roll(right_coef[k : k + 1, :], SLAB, 1))
        right = jnp.where(group == groups - 1, right, pltpu.roll(own, groups - 1, 0))
        up = jnp.where(
            spot < SLAB - 4,
            pltpu.roll(own, R - 4, 1),
            joined(pltpu.roll(above_coef, SLAB - 4 - 4 * k, 1)),
        )
        down = jnp.where(spot < 4, joined(pltpu.roll(below_coef, (R - 4 * k) % R, 1)), pltpu.roll(own, 4, 1))
        face[0, k] = 0.5 * (own + left)
        face[1, k] = 0.5 * (own + right)
        face[2, k] = 0.5 * (own + up)
        face[3, k] = 0.5 * (own + down)
        face[4, k] = 0.5 * (own + jnp.where(level < 3, pltpu.roll(own, R - 1, 1), 0.0))
        face[5, k] = 0.5 * (own + jnp.where(level > 0, pltpu.roll(own, 1, 1), 0.0))

    squares[...] = jnp.zeros_like(squares)
    lane = lax.broadcasted_iota(jnp.int32, (BLOCK, R), 1)
    inside = lane % SLAB
    depth = lane % 4

    def images(chunk, slot):
        for s in range(2):
            j = 2 * chunk + s
            weights = [[face[f, k, j : j + 1, :] for f in range(6)] for k in range(TERMS)]
            for start in range(0, R, BLOCK):
                rows = slice(start, start + BLOCK)
                v = turned[j + 1, rows, :]
                up = pltpu.roll(above[rows, :], (SLAB - 4 - 4 * j) % R, 1)
                down = pltpu.roll(below[rows, :], (R - 4 * j) % R, 1)
                steps = (
                    v - turned[j, rows, :],
                    v - turned[j + 2, rows, :],
                    v - jnp.where(inside < SLAB - 4, pltpu.roll(v, R - 4, 1), up),
                    v - jnp.where(inside < 4, down, pltpu.roll(v, 4, 1)),
                    v - jnp.where(depth < 3, pltpu.roll(v, R - 1, 1), 0.0),
                    v - jnp.where(depth > 0, pltpu.roll(v, 1, 1), 0.0),
                )
                summed_images = None
                for block in range(TERMS + 1):
                    if block == 0:
                        value = v
                    else:
                        k = block - 1
                        value = weights[k][0] * steps[0]
                        for weight, step in zip(weights[k][1:], steps[1:]):
                            value = value + weight * step
                        part = nominal_weights[k] * value
                        summed_images = part if summed_images is None else summed_images + part
                    high = value.astype(bf16)
                    rest = value - high.astype(f32)
                    squares[block, rows, :] += rest * rest
                    out = slice(block * R + start, block * R + start + BLOCK)
                    top[slot, out, s * R : (s + 1) * R] = high
                    bottom[slot, out, s * R : (s + 1) * R] = rest.astype(bf16)
                total[rows, :] = summed_images
            back = total[...].T
            nominal[j * SLAB : (j + 1) * SLAB, :] = back[0:SLAB]
            nominal[(j + groups) * SLAB : (j + groups + 1) * SLAB, :] = back[SLAB:]

    def grams(chunk, slot):
        for start in range(0, 2 * WIDTH, 256):
            rows = min(start + 256, WIDTH)
            if start + 256 <= WIDTH:
                right = top[slot, start : start + 256, :]
            elif start < WIDTH:
                right = jnp.concatenate([top[slot, start:WIDTH, :], bottom[slot, 0 : start + 256 - WIDTH, :]], axis=0)
            else:
                right = bottom[slot, start - WIDTH : start + 256 - WIDTH, :]
            value = lax.dot_general(
                top[slot, 0:rows, :], right, (((1,), (1,)), ((), ())), preferred_element_type=f32
            )
            if chunk == 0:
                product[0:rows, start : start + 256] = value
            else:
                product[0:rows, start : start + 256] += value

    chunks = groups // 2
    for chunk in range(chunks):
        images(chunk, chunk % 2)
        if chunk > 0:
            grams(chunk - 1, (chunk - 1) % 2)
    grams(chunks - 1, (chunks - 1) % 2)

    r = lax.broadcasted_iota(jnp.int32, (R, R), 0)
    c = lax.broadcasted_iota(jnp.int32, (R, R), 1)

    def gram(a, b):
        high = product[a * R : (a + 1) * R, b * R : (b + 1) * R]
        one = product[a * R : (a + 1) * R, WIDTH + b * R : WIDTH + (b + 1) * R]
        two = product[b * R : (b + 1) * R, WIDTH + a * R : WIDTH + (a + 1) * R]
        if a != b:
            return high + one, two
        return high + one + jnp.where(r == c, jnp.sum(squares[a], axis=1, keepdims=True), 0.0), two

    def symmetric(a, b):
        one, two = gram(a, b)
        return one + two.T

    def diagonal(matrix):
        return jnp.sum(jnp.where(c == r, matrix, 0.0), axis=0, keepdims=True)

    base = symmetric(0, 0)
    for h, (even, full) in enumerate(halves):
        zero, one, two, three = [symmetric(*pair) for pair in even]
        tiles = [jnp.where(c >= r, base, zero), jnp.where(c >= r, one, two), jnp.where(c >= r, three, 0.0)]
        lines = []
        for line in (diagonal(zero), diagonal(two)):
            lines += [line, pltpu.roll(line, SLAB, 1)]
        for q, line in enumerate(lines):
            tiles[2] = jnp.where((r == R - 1 - q) & (c < SLAB), line, tiles[2])
        for pair in full:
            high, low = gram(*pair)
            tiles.append(high.T + low)

        def store(target, tiles=tiles):
            for q, tile in enumerate(tiles):
                target[q * R : (q + 1) * R, :] = tile

        pl.when(me[0] == h)(lambda: store(mine))
        pl.when(me[0] != h)(lambda: store(other))


def spread(value):
    return jnp.broadcast_to(value, (8, R))


def stacked(values, row8):
    out = values[-1]
    for i in range(len(values) - 2, -1, -1):
        out = jnp.where(row8 == i, values[i], out)
    return out


def panel_factor(rows, start):
    column = [spread(rows[:, start + l : start + l + 1]) for l in range(8)]
    a = [[spread(column[l][i : i + 1, :]) for l in range(i + 1)] for i in range(8)]
    inverse_pivot = [None] * 8
    lower = [[None] * 8 for _ in range(8)]
    for j in range(8):
        inverse_pivot[j] = 1.0 / a[j][j]
        for i in range(j + 1, 8):
            lower[i][j] = a[i][j] * inverse_pivot[j]
        for i in range(j + 1, 8):
            for l in range(j + 1, i + 1):
                a[i][l] = a[i][l] - lower[i][j] * a[l][j]
    turn = [[None] * 8 for _ in range(8)]
    for j in range(8):
        for i in range(j + 1, 8):
            value = lower[i][j]
            for l in range(j + 1, i):
                value = value + lower[i][l] * turn[l][j]
            turn[i][j] = -value
    return [a[j][j] for j in range(8)], inverse_pivot, turn


def factor_kernel(slot, inverse_t, inverse, *, cells):
    r = lax.broadcasted_iota(jnp.int32, (R, R), 0)
    c = lax.broadcasted_iota(jnp.int32, (R, R), 1)
    gram = jnp.where(c >= r, slot[...], slot[...].T) * (1.0 / cells)
    row8 = lax.broadcasted_iota(jnp.int32, (8, R), 0)
    lane8 = lax.broadcasted_iota(jnp.int32, (8, R), 1)
    panels = R // 8
    left = [gram[8 * i : 8 * i + 8, :] for i in range(panels)]
    right = [jnp.where(row8 + 8 * i == lane8, 1.0, 0.0).astype(f32) for i in range(panels)]
    for p in range(panels):
        start = 8 * p
        pivots, inverse_pivots, turn = panel_factor(left[p], start)
        ends = []
        for rows in (left[p], right[p]):
            out = rows
            for l in range(7):
                weight = jnp.where(row8 > l, turn[7][l], 0.0)
                for i in range(l + 1, 7):
                    weight = jnp.where(row8 == i, turn[i][l], weight)
                out = out + weight * spread(rows[l : l + 1, :])
            ends.append(out)
        inverse[start : start + 8, :] = ends[1] * stacked([1.0 / jnp.sqrt(pivot) for pivot in pivots], row8)
        if p == panels - 1:
            break
        scale = stacked(inverse_pivots, row8)
        solved = []
        for rows in ends:
            rows = rows * scale
            out = rows
            for i in range(1, 8):
                weight = jnp.where(row8 == 0, turn[i][0], 0.0)
                for l in range(1, i):
                    weight = jnp.where(row8 == l, turn[i][l], weight)
                out = out + weight * spread(rows[i : i + 1, :])
            solved.append(out)
        weights = [spread(left[p + 1][:, start + l : start + l + 1]) for l in range(8)]
        rest = left[p + 2 :]
        updates = []
        for out in solved:
            terms = [weights[l] * spread(out[l : l + 1, :]) for l in range(8)]
            while len(terms) > 1:
                terms = [terms[i] + terms[i + 1] for i in range(0, len(terms), 2)]
            updates.append(terms[0])
        left[p + 1] = left[p + 1] - updates[0]
        right[p + 1] = right[p + 1] - updates[1]
        if rest:
            columns = jnp.concatenate(rest, axis=0)[:, start : start + 8]
            update = jnp.dot(columns, jnp.concatenate(solved, axis=1), precision=HIGHEST, preferred_element_type=f32)
            for i in range(p + 2, panels):
                q = 8 * (i - p - 2)
                left[i] = left[i] - update[q : q + 8, :R]
                right[i] = right[i] - update[q : q + 8, R:]
    inverse_t[...] = inverse[...].T


def parts(value, count):
    out = []
    for _ in range(count):
        out.append(value.astype(bf16))
        value = value - out[-1].astype(f32)
    return out


def finish_kernel(
    me, mine, other, basis, nominal, inverse_t, ortho_out, nominal_out, reduced_out, residual_out, packed, *, cells
):
    packed[pl.ds(pl.multiple_of(me[0] * HALF, R), HALF), :] = mine[...]
    packed[pl.ds(pl.multiple_of((1 - me[0]) * HALF, R), HALF), :] = other[...]
    high, middle, low = parts(inverse_t[...], 3)
    line = jnp.concatenate([high, middle], axis=1)
    square = jnp.concatenate([line, line], axis=0)
    last = jnp.concatenate([high, low], axis=0)

    def short(value):
        one, two = parts(value, 2)
        out = jnp.dot(jnp.concatenate([one, two], axis=1), square, preferred_element_type=f32)
        return out[:, :R] + out[:, R:]

    def product(value):
        one, two, three = parts(value, 3)
        out = jnp.dot(jnp.concatenate([one, two], axis=1), square, preferred_element_type=f32)
        end = jnp.dot(jnp.concatenate([three, one], axis=1), last, preferred_element_type=f32)
        return out[:, :R] + (out[:, R:] + end)

    step = 512
    for source, target in ((basis, ortho_out), (nominal, nominal_out)):
        for start in range(0, basis.shape[0], step):
            target[start : start + step, :] = short(source[start : start + step, :])

    r = lax.broadcasted_iota(jnp.int32, (R, R), 0)
    c = lax.broadcasted_iota(jnp.int32, (R, R), 1)
    scale = 1.0 / cells

    def moved(matrix):
        return product(product(matrix * scale).T)

    for h, (even, full) in enumerate(halves):
        tiles = [packed[h * HALF + q * R : h * HALF + (q + 1) * R, :] for q in range(HALF_SLOTS)]
        turned = [tile.T for tile in tiles[:3]]
        lines = []
        for q in range(2):
            one = tiles[2][R - 1 - 2 * q : R - 2 * q, :]
            two = pltpu.roll(tiles[2][R - 2 - 2 * q : R - 1 - 2 * q, :], SLAB, 1)
            lines.append(jnp.where(c[0:1] < SLAB, one, two))
        matrices = [
            jnp.where(c < r, tiles[0], jnp.where(c == r, lines[0], turned[0])),
            jnp.where(c >= r, tiles[1], turned[1]),
            jnp.where(c < r, tiles[1], jnp.where(c == r, lines[1], turned[1])),
            jnp.where(c >= r, tiles[2], turned[2]),
        ] + tiles[3:]
        for (a, b), matrix in zip(even + full, matrices):
            if a == 0:
                reduced_out[b - 1] = moved(matrix)
            else:
                residual_out[operator_pairs.index((a - 1, b - 1))] = moved(matrix)


def summed(values, groups):
    count = lax.axis_size("gx")
    width = values.shape[1]
    parts = values.reshape(count, -1, width)
    shard = jnp.sum(lax.all_to_all(parts, "gx", 0, 0), axis=0)
    depth = len(groups[0])
    along = jnp.broadcast_to(shard[None], (depth,) + shard.shape)
    shard = jnp.sum(lax.all_to_all(along, "gy", 0, 0, axis_index_groups=groups), axis=0)
    spread = jnp.broadcast_to(shard[None], (count,) + shard.shape)
    return lax.all_to_all(spread, "gx", 0, 0).reshape(values.shape)


def shards(raw_basis, coefficients, nominal_weights):
    nx, ny, nz, width = raw_basis.shape
    count_x, count_y = lax.axis_size("gx"), lax.axis_size("gy")
    cells = nx * ny * nz * count_x * count_y
    flat = raw_basis.reshape(-1, width)
    coef = jnp.transpose(coefficients, (0, 2, 3, 1)).reshape(-1, nx)
    vmem = pl.BlockSpec(memory_space=pltpu.VMEM)
    smem = pl.BlockSpec(memory_space=pltpu.SMEM)

    def array(*shape):
        return jax.ShapeDtypeStruct(shape, f32)

    y_rows = 4 * nx + 4 * TERMS
    x_low, x_high, y_low, y_high = pl.pallas_call(
        faces_kernel,
        out_shape=(array(2 * SLAB, R), array(2 * SLAB, R), array(y_rows, R), array(y_rows, R)),
        in_specs=[vmem, vmem],
        out_specs=(vmem,) * 4,
        name="faces",
    )(flat, coef)
    up_x = [(i, i + 1) for i in range(count_x - 1)]
    up_y = [(i, i + 1) for i in range(count_y - 1)]
    from_left = lax.ppermute(x_high, "gx", up_x)
    from_right = lax.ppermute(x_low, "gx", [(b, a) for a, b in up_x])
    from_below = lax.ppermute(y_high, "gy", up_y)
    from_above = lax.ppermute(y_low, "gy", [(b, a) for a, b in up_y])

    me = (lax.axis_index("gy") % 2).astype(jnp.int32).reshape(1)
    groups = nx // 2
    mine, other, raw_nominal = pl.pallas_call(
        images_kernel,
        out_shape=(array(HALF, R), array(HALF, R), array(nx * SLAB, R)),
        in_specs=[smem, smem] + [vmem] * 6,
        out_specs=(vmem,) * 3,
        scratch_shapes=[
            pltpu.VMEM((groups + 2, R, R), f32),
            pltpu.VMEM((R, 4 * nx), f32),
            pltpu.VMEM((R, 4 * nx), f32),
            pltpu.VMEM((6, TERMS, groups, R), f32),
            pltpu.VMEM((2, WIDTH, 2 * R), bf16),
            pltpu.VMEM((2, WIDTH, 2 * R), bf16),
            pltpu.VMEM((WIDTH, 2 * WIDTH), f32),
            pltpu.VMEM((TERMS + 1, R, R), f32),
            pltpu.VMEM((R, R), f32),
        ],
        name="images",
    )(me, nominal_weights, flat, coef, from_left, from_right, from_below, from_above)

    swap = [(i, i ^ 1) for i in range(count_y)]
    along_z = [list(range(core, count_y, 2)) for core in range(2)]
    mine = mine + lax.ppermute(other, "gy", swap)
    mine = summed(mine, along_z)
    other = lax.ppermute(mine, "gy", swap)

    def factor(*refs):
        factor_kernel(*refs, cells=cells)

    def finish(*refs):
        finish_kernel(*refs, cells=cells)

    inverse_t = pl.pallas_call(
        factor,
        out_shape=array(R, R),
        grid=(1,),
        in_specs=[pl.BlockSpec((R, R), lambda i: (0, 0))],
        out_specs=pl.BlockSpec((R, R), lambda i: (0, 0)),
        scratch_shapes=[pltpu.VMEM((R, R), f32)],
        name="factor",
    )(mine)
    ortho, nominal, reduced_ops, residual_grams = pl.pallas_call(
        finish,
        out_shape=(array(nx * SLAB, R), array(nx * SLAB, R), array(TERMS, R, R), array(len(operator_pairs), R, R)),
        in_specs=[smem] + [vmem] * 5,
        out_specs=(vmem,) * 4,
        scratch_shapes=[pltpu.VMEM((2 * HALF, R), f32)],
        name="finish",
    )(me, mine, other, flat, raw_nominal, inverse_t)
    shape = raw_basis.shape
    return (ortho.reshape(shape), nominal.reshape(shape), reduced_ops, residual_grams)


def solution(mesh):
    in_specs = (P("gx", "gy", None, None), P(None, "gx", "gy", None), P())
    out_specs = (P("gx", "gy", None, None), P("gx", "gy", None, None), P(), P())
    return jax.shard_map(shards, mesh=mesh, in_specs=in_specs, out_specs=out_specs, check_vma=False)
```

```python
import jax
import jax.numpy as jnp
from jax import lax
from jax.experimental import pallas as pl
from jax.experimental.pallas import tpu as pltpu
from jax.sharding import PartitionSpec as P

R = 128
TERMS = 4
operator_pairs = ((0, 0), (0, 1), (0, 2), (0, 3), (1, 1), (1, 2), (1, 3), (2, 2), (2, 3), (3, 3))
crossed_pairs = tuple(pair for pair in operator_pairs if pair[0] != pair[1])
HIGHEST = lax.Precision.HIGHEST
f32, bf16 = jnp.float32, jnp.bfloat16

HALF_SLOTS = 6
HALF = HALF_SLOTS * R
SLAB = 64
WIDTH = (TERMS + 1) * R
BLOCK = 32
VMEM_LIMIT = 24 * 2**20
halves = (
    ([(0, k + 1) for k in range(TERMS)], [(a + 1, b + 1) for a, b in crossed_pairs[:3]]),
    ([(k + 1, k + 1) for k in range(TERMS)], [(a + 1, b + 1) for a, b in crossed_pairs[3:]]),
)

def faces_kernel(me, basis, coef, x_first, x_second, y_first, y_second):
    lane = lax.broadcasted_iota(jnp.int32, (SLAB, R), 1)
    slabs = basis.shape[0] // SLAB

    def x_faces(low, high):
        low[0:SLAB, :] = basis[0:SLAB, :]
        high[0:SLAB, :] = basis[(slabs - 1) * SLAB : slabs * SLAB, :]
        first = jnp.zeros((SLAB, R), f32)
        last = jnp.zeros((SLAB, R), f32)
        for k in range(TERMS):
            rows = coef[k * SLAB : (k + 1) * SLAB, :]
            first = jnp.where(lane == k, rows[:, 0:1], first)
            last = jnp.where(lane == k, rows[:, slabs - 1 : slabs], last)
        low[SLAB : 2 * SLAB, :] = first
        high[SLAB : 2 * SLAB, :] = last

    def y_faces(low, high):
        for x in range(slabs):
            low[4 * x : 4 * x + 4, :] = basis[x * SLAB : x * SLAB + 4, :]
            high[4 * x : 4 * x + 4, :] = basis[x * SLAB + SLAB - 4 : (x + 1) * SLAB, :]
        low[4 * slabs :, :] = jnp.zeros((16, R), f32)
        high[4 * slabs :, :] = jnp.zeros((16, R), f32)
        for k in range(TERMS):
            low[4 * (slabs + k) : 4 * (slabs + k) + 4, 0:slabs] = coef[k * SLAB : k * SLAB + 4, :]
            high[4 * (slabs + k) : 4 * (slabs + k) + 4, 0:slabs] = coef[(k + 1) * SLAB - 4 : (k + 1) * SLAB, :]

    pl.when(me[1] == 0)(lambda: x_faces(x_second, x_first))
    pl.when(me[1] != 0)(lambda: x_faces(x_first, x_second))
    pl.when(me[0] == 0)(lambda: y_faces(y_second, y_first))
    pl.when(me[0] != 0)(lambda: y_faces(y_first, y_second))


def turn_kernel(basis, turned):
    groups = turned.shape[0]
    for j in range(groups):
        one = basis[j * SLAB : (j + 1) * SLAB, :]
        two = basis[(j + groups) * SLAB : (j + groups + 1) * SLAB, :]
        turned[j] = jnp.concatenate([one, two], axis=0).T


def images_kernel(
    me, nominal_weights, turned, before, after, coef, x_first, x_second, y_first, y_second, mine, other, nominal,
    from_left, from_right, from_below, from_above, ends, above, below, face, top, bottom, product, squares, total,
):
    groups = turned.shape[0]
    slabs = 2 * groups

    def copied(*pairs):
        for source, target in pairs:
            target[...] = source[...]

    pl.when(me[1] == 0)(lambda: copied((x_second, from_left), (x_first, from_right)))
    pl.when(me[1] != 0)(lambda: copied((x_first, from_left), (x_second, from_right)))
    pl.when(me[0] == 0)(lambda: copied((y_second, from_below), (y_first, from_above)))
    pl.when(me[0] != 0)(lambda: copied((y_first, from_below), (y_second, from_above)))

    ends[0] = jnp.concatenate([from_left[0:SLAB, :], before[...]], axis=0).T
    ends[1] = jnp.concatenate([after[...], from_right[0:SLAB, :]], axis=0).T

    def strip(j, rows):
        if j < 0:
            return ends[0, rows, :]
        if j == groups:
            return ends[1, rows, :]
        return turned[j, rows, :]

    above[...] = from_above[0 : 4 * slabs, :].T
    below[...] = from_below[0 : 4 * slabs, :].T

    spot = lax.broadcasted_iota(jnp.int32, (groups, R), 1) % SLAB
    first = lax.broadcasted_iota(jnp.int32, (groups, R), 1) < SLAB
    group = lax.broadcasted_iota(jnp.int32, (groups, R), 0)
    level = spot % 4

    def joined(rows):
        return jnp.where(first, rows[0:groups], pltpu.roll(rows[groups:slabs], SLAB, 1))

    def flipped(tile):
        return jnp.concatenate([tile, jnp.zeros((R - tile.shape[0], R), f32)], axis=0).T

    left_coef = flipped(from_left[SLAB : 2 * SLAB, :])
    right_coef = flipped(from_right[SLAB : 2 * SLAB, :])
    above_coef = flipped(from_above[4 * slabs :, :])
    below_coef = flipped(from_below[4 * slabs :, :])
    for k in range(TERMS):
        rows = jnp.concatenate([coef[k * SLAB : (k + 1) * SLAB, :], jnp.zeros((SLAB, R - slabs), f32)], axis=1)
        own = joined(flipped(rows))
        half = pltpu.roll(own, SLAB, 1)
        left = jnp.where(first, left_coef[k : k + 1, :], half[groups - 1 : groups, :])
        left = jnp.where(group == 0, left, pltpu.roll(own, 1, 0))
        right = jnp.where(first, half[0:1, :], pltpu.roll(right_coef[k : k + 1, :], SLAB, 1))
        right = jnp.where(group == groups - 1, right, pltpu.roll(own, groups - 1, 0))
        up = jnp.where(
            spot < SLAB - 4,
            pltpu.roll(own, R - 4, 1),
            joined(pltpu.roll(above_coef, SLAB - 4 - 4 * k, 1)),
        )
        down = jnp.where(spot < 4, joined(pltpu.roll(below_coef, (R - 4 * k) % R, 1)), pltpu.roll(own, 4, 1))
        face[0, k] = 0.5 * (own + left)
        face[1, k] = 0.5 * (own + right)
        face[2, k] = 0.5 * (own + up)
        face[3, k] = 0.5 * (own + down)
        face[4, k] = 0.5 * (own + jnp.where(level < 3, pltpu.roll(own, R - 1, 1), 0.0))
        face[5, k] = 0.5 * (own + jnp.where(level > 0, pltpu.roll(own, 1, 1), 0.0))

    squares[...] = jnp.zeros_like(squares)
    lane = lax.broadcasted_iota(jnp.int32, (BLOCK, R), 1)
    inside = lane % SLAB
    depth = lane % 4

    def images(chunk, slot):
        for s in range(2):
            j = 2 * chunk + s
            weights = [[face[f, k, j : j + 1, :] for f in range(6)] for k in range(TERMS)]
            for start in range(0, R, BLOCK):
                rows = slice(start, start + BLOCK)
                v = turned[j, rows, :]
                up = pltpu.roll(above[rows, :], (SLAB - 4 - 4 * j) % R, 1)
                down = pltpu.roll(below[rows, :], (R - 4 * j) % R, 1)
                steps = (
                    v - strip(j - 1, rows),
                    v - strip(j + 1, rows),
                    v - jnp.where(inside < SLAB - 4, pltpu.roll(v, R - 4, 1), up),
                    v - jnp.where(inside < 4, down, pltpu.roll(v, 4, 1)),
                    v - jnp.where(depth < 3, pltpu.roll(v, R - 1, 1), 0.0),
                    v - jnp.where(depth > 0, pltpu.roll(v, 1, 1), 0.0),
                )
                summed_images = None
                for block in range(TERMS + 1):
                    if block == 0:
                        value = v
                    else:
                        k = block - 1
                        value = weights[k][0] * steps[0]
                        for weight, step in zip(weights[k][1:], steps[1:]):
                            value = value + weight * step
                        part = nominal_weights[k] * value
                        summed_images = part if summed_images is None else summed_images + part
                    high = value.astype(bf16)
                    rest = value - high.astype(f32)
                    squares[block, rows, :] += rest * rest
                    out = slice(block * R + start, block * R + start + BLOCK)
                    top[slot, out, s * R : (s + 1) * R] = high
                    bottom[slot, out, s * R : (s + 1) * R] = rest.astype(bf16)
                total[rows, :] = summed_images
            back = total[...].T
            nominal[j * SLAB : (j + 1) * SLAB, :] = back[0:SLAB]
            nominal[(j + groups) * SLAB : (j + groups + 1) * SLAB, :] = back[SLAB:]

    def grams(chunk, slot):
        for start in range(0, 2 * WIDTH, 256):
            rows = min(start + 256, WIDTH)
            if start + 256 <= WIDTH:
                right = top[slot, start : start + 256, :]
            elif start < WIDTH:
                right = jnp.concatenate([top[slot, start:WIDTH, :], bottom[slot, 0 : start + 256 - WIDTH, :]], axis=0)
            else:
                right = bottom[slot, start - WIDTH : start + 256 - WIDTH, :]
            value = lax.dot_general(
                top[slot, 0:rows, :], right, (((1,), (1,)), ((), ())), preferred_element_type=f32
            )
            if chunk == 0:
                product[0:rows, start : start + 256] = value
            else:
                product[0:rows, start : start + 256] += value

    chunks = groups // 2
    for chunk in range(chunks):
        images(chunk, chunk % 2)
        if chunk > 0:
            grams(chunk - 1, (chunk - 1) % 2)
    grams(chunks - 1, (chunks - 1) % 2)

    r = lax.broadcasted_iota(jnp.int32, (R, R), 0)
    c = lax.broadcasted_iota(jnp.int32, (R, R), 1)

    def gram(a, b):
        high = product[a * R : (a + 1) * R, b * R : (b + 1) * R]
        one = product[a * R : (a + 1) * R, WIDTH + b * R : WIDTH + (b + 1) * R]
        two = product[b * R : (b + 1) * R, WIDTH + a * R : WIDTH + (a + 1) * R]
        if a != b:
            return high + one, two
        return high + one + jnp.where(r == c, jnp.sum(squares[a], axis=1, keepdims=True), 0.0), two

    def symmetric(a, b):
        one, two = gram(a, b)
        return one + two.T

    def diagonal(matrix):
        return jnp.sum(jnp.where(c == r, matrix, 0.0), axis=0, keepdims=True)

    base = symmetric(0, 0)
    for h, (even, full) in enumerate(halves):
        zero, one, two, three = [symmetric(*pair) for pair in even]
        tiles = [jnp.where(c >= r, base, zero), jnp.where(c >= r, one, two), jnp.where(c >= r, three, 0.0)]
        lines = []
        for line in (diagonal(zero), diagonal(two)):
            lines += [line, pltpu.roll(line, SLAB, 1)]
        for q, line in enumerate(lines):
            tiles[2] = jnp.where((r == R - 1 - q) & (c < SLAB), line, tiles[2])
        for pair in full:
            high, low = gram(*pair)
            tiles.append(high.T + low)

        def store(target, tiles=tiles):
            for q, tile in enumerate(tiles):
                target[q * R : (q + 1) * R, :] = tile

        pl.when(me[0] == h)(lambda: store(mine))
        pl.when(me[0] != h)(lambda: store(other))


def spread(value):
    return jnp.broadcast_to(value, (8, R))


def stacked(values, row8):
    out = values[-1]
    for i in range(len(values) - 2, -1, -1):
        out = jnp.where(row8 == i, values[i], out)
    return out


def panel_factor(rows, start):
    column = [spread(rows[:, start + l : start + l + 1]) for l in range(8)]
    a = [[spread(column[l][i : i + 1, :]) for l in range(i + 1)] for i in range(8)]
    inverse_pivot = [None] * 8
    lower = [[None] * 8 for _ in range(8)]
    for j in range(8):
        inverse_pivot[j] = 1.0 / a[j][j]
        for i in range(j + 1, 8):
            lower[i][j] = a[i][j] * inverse_pivot[j]
        for i in range(j + 1, 8):
            for l in range(j + 1, i + 1):
                a[i][l] = a[i][l] - lower[i][j] * a[l][j]
    turn = [[None] * 8 for _ in range(8)]
    for j in range(8):
        for i in range(j + 1, 8):
            value = lower[i][j]
            for l in range(j + 1, i):
                value = value + lower[i][l] * turn[l][j]
            turn[i][j] = -value
    return [a[j][j] for j in range(8)], inverse_pivot, turn


def factor_kernel(slot, inverse_t, inverse, *, cells):
    r = lax.broadcasted_iota(jnp.int32, (R, R), 0)
    c = lax.broadcasted_iota(jnp.int32, (R, R), 1)
    gram = jnp.where(c >= r, slot[...], slot[...].T) * (1.0 / cells)
    row8 = lax.broadcasted_iota(jnp.int32, (8, R), 0)
    lane8 = lax.broadcasted_iota(jnp.int32, (8, R), 1)
    panels = R // 8
    left = [gram[8 * i : 8 * i + 8, :] for i in range(panels)]
    right = [jnp.where(row8 + 8 * i == lane8, 1.0, 0.0).astype(f32) for i in range(panels)]
    for p in range(panels):
        start = 8 * p
        pivots, inverse_pivots, turn = panel_factor(left[p], start)
        ends = []
        for rows in (left[p], right[p]):
            out = rows
            for l in range(7):
                weight = jnp.where(row8 > l, turn[7][l], 0.0)
                for i in range(l + 1, 7):
                    weight = jnp.where(row8 == i, turn[i][l], weight)
                out = out + weight * spread(rows[l : l + 1, :])
            ends.append(out)
        inverse[start : start + 8, :] = ends[1] * stacked([1.0 / jnp.sqrt(pivot) for pivot in pivots], row8)
        if p == panels - 1:
            break
        scale = stacked(inverse_pivots, row8)
        solved = []
        for rows in ends:
            rows = rows * scale
            out = rows
            for i in range(1, 8):
                weight = jnp.where(row8 == 0, turn[i][0], 0.0)
                for l in range(1, i):
                    weight = jnp.where(row8 == l, turn[i][l], weight)
                out = out + weight * spread(rows[i : i + 1, :])
            solved.append(out)
        weights = [spread(left[p + 1][:, start + l : start + l + 1]) for l in range(8)]
        rest = left[p + 2 :]
        updates = []
        for out in solved:
            terms = [weights[l] * spread(out[l : l + 1, :]) for l in range(8)]
            while len(terms) > 1:
                terms = [terms[i] + terms[i + 1] for i in range(0, len(terms), 2)]
            updates.append(terms[0])
        left[p + 1] = left[p + 1] - updates[0]
        right[p + 1] = right[p + 1] - updates[1]
        if rest:
            columns = jnp.concatenate(rest, axis=0)[:, start : start + 8]
            update = jnp.dot(columns, jnp.concatenate(solved, axis=1), precision=HIGHEST, preferred_element_type=f32)
            for i in range(p + 2, panels):
                q = 8 * (i - p - 2)
                left[i] = left[i] - update[q : q + 8, :R]
                right[i] = right[i] - update[q : q + 8, R:]
    inverse_t[...] = inverse[...].T


def parts(value, count):
    out = []
    for _ in range(count):
        out.append(value.astype(bf16))
        value = value - out[-1].astype(f32)
    return out


def finish_kernel(
    me, mine, other, basis, nominal, inverse_t, ortho_out, nominal_out, reduced_out, residual_out, packed, *, cells
):
    packed[pl.ds(pl.multiple_of(me[0] * HALF, R), HALF), :] = mine[...]
    packed[pl.ds(pl.multiple_of((1 - me[0]) * HALF, R), HALF), :] = other[...]
    high, middle, low = parts(inverse_t[...], 3)
    line = jnp.concatenate([high, middle], axis=1)
    square = jnp.concatenate([line, line], axis=0)
    last = jnp.concatenate([high, low], axis=0)

    def short(value):
        one, two = parts(value, 2)
        out = jnp.dot(jnp.concatenate([one, two], axis=1), square, preferred_element_type=f32)
        return out[:, :R] + out[:, R:]

    def product(value):
        one, two, three = parts(value, 3)
        out = jnp.dot(jnp.concatenate([one, two], axis=1), square, preferred_element_type=f32)
        end = jnp.dot(jnp.concatenate([three, one], axis=1), last, preferred_element_type=f32)
        return out[:, :R] + (out[:, R:] + end)

    step = 512
    for source, target in ((basis, ortho_out), (nominal, nominal_out)):
        for start in range(0, basis.shape[0], step):
            target[start : start + step, :] = short(source[start : start + step, :])

    r = lax.broadcasted_iota(jnp.int32, (R, R), 0)
    c = lax.broadcasted_iota(jnp.int32, (R, R), 1)
    scale = 1.0 / cells

    def moved(matrix):
        return product(product(matrix * scale).T)

    for h, (even, full) in enumerate(halves):
        tiles = [packed[h * HALF + q * R : h * HALF + (q + 1) * R, :] for q in range(HALF_SLOTS)]
        turned = [tile.T for tile in tiles[:3]]
        lines = []
        for q in range(2):
            one = tiles[2][R - 1 - 2 * q : R - 2 * q, :]
            two = pltpu.roll(tiles[2][R - 2 - 2 * q : R - 1 - 2 * q, :], SLAB, 1)
            lines.append(jnp.where(c[0:1] < SLAB, one, two))
        matrices = [
            jnp.where(c < r, tiles[0], jnp.where(c == r, lines[0], turned[0])),
            jnp.where(c >= r, tiles[1], turned[1]),
            jnp.where(c < r, tiles[1], jnp.where(c == r, lines[1], turned[1])),
            jnp.where(c >= r, tiles[2], turned[2]),
        ] + tiles[3:]
        for (a, b), matrix in zip(even + full, matrices):
            if a == 0:
                reduced_out[b - 1] = moved(matrix)
            else:
                residual_out[operator_pairs.index((a - 1, b - 1))] = moved(matrix)


def summed(values, groups):
    count = lax.axis_size("gx")
    width = values.shape[1]
    parts = values.reshape(count, -1, width)
    shard = jnp.sum(lax.all_to_all(parts, "gx", 0, 0), axis=0)
    depth = len(groups[0])
    along = jnp.broadcast_to(shard[None], (depth,) + shard.shape)
    shard = jnp.sum(lax.all_to_all(along, "gy", 0, 0, axis_index_groups=groups), axis=0)
    spread = jnp.broadcast_to(shard[None], (count,) + shard.shape)
    return lax.all_to_all(spread, "gx", 0, 0).reshape(values.shape)


def shards(raw_basis, coefficients, nominal_weights):
    nx, ny, nz, width = raw_basis.shape
    count_x, count_y = lax.axis_size("gx"), lax.axis_size("gy")
    cells = nx * ny * nz * count_x * count_y
    flat = raw_basis.reshape(-1, width)
    coef = jnp.transpose(coefficients, (0, 2, 3, 1)).reshape(-1, nx)
    vmem = pl.BlockSpec(memory_space=pltpu.VMEM)
    smem = pl.BlockSpec(memory_space=pltpu.SMEM)

    def array(*shape):
        return jax.ShapeDtypeStruct(shape, f32)

    me = jnp.stack([lax.axis_index("gy") % 2, lax.axis_index("gx") % 2]).astype(jnp.int32)
    small = pltpu.CompilerParams(vmem_limit_bytes=VMEM_LIMIT)
    y_rows = 4 * nx + 4 * TERMS
    faces = pl.pallas_call(
        faces_kernel,
        out_shape=(array(2 * SLAB, R), array(2 * SLAB, R), array(y_rows, R), array(y_rows, R)),
        in_specs=[smem, vmem, vmem],
        out_specs=(vmem,) * 4,
        compiler_params=small,
        name="faces",
    )(me, flat, coef)

    def swaps(first, count):
        pairs = [(i, i + 1) for i in range(first, count - 1, 2)]
        return pairs + [(b, a) for a, b in pairs]

    halos = [
        lax.ppermute(face, axis, swaps(first, count))
        for face, axis, first, count in zip(faces, ("gx", "gx", "gy", "gy"), (0, 1, 0, 1), (count_x, count_x, count_y, count_y))
    ]
    groups = nx // 2
    turned = pl.pallas_call(
        turn_kernel,
        out_shape=array(groups, R, R),
        in_specs=[vmem],
        out_specs=vmem,
        compiler_params=small,
        name="turn",
    )(flat)

    mine, other, raw_nominal = pl.pallas_call(
        images_kernel,
        out_shape=(array(HALF, R), array(HALF, R), array(nx * SLAB, R)),
        grid=(1,),
        in_specs=[smem, smem, vmem]
        + [pl.BlockSpec((SLAB, R), lambda i, at=at: (at, 0)) for at in (groups - 1, groups)]
        + [vmem] * 5,
        out_specs=(vmem,) * 3,
        scratch_shapes=[
            pltpu.VMEM((2 * SLAB, R), f32),
            pltpu.VMEM((2 * SLAB, R), f32),
            pltpu.VMEM((y_rows, R), f32),
            pltpu.VMEM((y_rows, R), f32),
            pltpu.VMEM((2, R, R), f32),
            pltpu.VMEM((R, 4 * nx), f32),
            pltpu.VMEM((R, 4 * nx), f32),
            pltpu.VMEM((6, TERMS, groups, R), f32),
            pltpu.VMEM((2, WIDTH, 2 * R), bf16),
            pltpu.VMEM((2, WIDTH, 2 * R), bf16),
            pltpu.VMEM((WIDTH, 2 * WIDTH), f32),
            pltpu.VMEM((TERMS + 1, R, R), f32),
            pltpu.VMEM((R, R), f32),
        ],
        compiler_params=small,
        name="images",
    )(me, nominal_weights, turned, flat, flat, coef, *halos)

    swap = [(i, i ^ 1) for i in range(count_y)]
    along_z = [list(range(core, count_y, 2)) for core in range(2)]
    mine = mine + lax.ppermute(other, "gy", swap)
    mine = summed(mine, along_z)
    other = lax.ppermute(mine, "gy", swap)

    def factor(*refs):
        factor_kernel(*refs, cells=cells)

    def finish(*refs):
        finish_kernel(*refs, cells=cells)

    inverse_t = pl.pallas_call(
        factor,
        out_shape=array(R, R),
        grid=(1,),
        in_specs=[pl.BlockSpec((R, R), lambda i: (0, 0))],
        out_specs=pl.BlockSpec((R, R), lambda i: (0, 0)),
        scratch_shapes=[pltpu.VMEM((R, R), f32)],
        compiler_params=small,
        name="factor",
    )(mine)
    ortho, nominal, reduced_ops, residual_grams = pl.pallas_call(
        finish,
        out_shape=(array(nx * SLAB, R), array(nx * SLAB, R), array(TERMS, R, R), array(len(operator_pairs), R, R)),
        in_specs=[smem] + [vmem] * 5,
        out_specs=(vmem,) * 4,
        scratch_shapes=[pltpu.VMEM((2 * HALF, R), f32)],
        compiler_params=small,
        name="finish",
    )(me, mine, other, flat, raw_nominal, inverse_t)
    shape = raw_basis.shape
    return (ortho.reshape(shape), nominal.reshape(shape), reduced_ops, residual_grams)


def solution(mesh):
    in_specs = (P("gx", "gy", None, None), P(None, "gx", "gy", None), P())
    out_specs = (P("gx", "gy", None, None), P("gx", "gy", None, None), P(), P())
    return jax.shard_map(shards, mesh=mesh, in_specs=in_specs, out_specs=out_specs, check_vma=False)
```

```python
import jax
import jax.numpy as jnp
from jax import lax
from jax.experimental import pallas as pl
from jax.experimental.pallas import tpu as pltpu
from jax.sharding import PartitionSpec as P

R = 128
TERMS = 4
operator_pairs = ((0, 0), (0, 1), (0, 2), (0, 3), (1, 1), (1, 2), (1, 3), (2, 2), (2, 3), (3, 3))
crossed_pairs = tuple(pair for pair in operator_pairs if pair[0] != pair[1])
HIGHEST = lax.Precision.HIGHEST
f32, bf16 = jnp.float32, jnp.bfloat16

HALF_SLOTS = 6
HALF = HALF_SLOTS * R
SLAB = 64
WIDTH = (TERMS + 1) * R
BLOCK = 32
STEP = 4
VMEM_LIMIT = 24 * 2**20
halves = (
    ([(0, k + 1) for k in range(TERMS)], [(a + 1, b + 1) for a, b in crossed_pairs[:3]]),
    ([(k + 1, k + 1) for k in range(TERMS)], [(a + 1, b + 1) for a, b in crossed_pairs[3:]]),
)

def faces_kernel(me, basis, coef_in, x_first, x_second, y_first, y_second, x_low, x_high, y_low, y_high, coef, sems):
    lane = lax.broadcasted_iota(jnp.int32, (SLAB, R), 1)
    slabs = basis.shape[0]
    copies = [
        pltpu.make_async_copy(coef_in, coef, sems.at[0]),
        pltpu.make_async_copy(basis.at[0], x_low, sems.at[1]),
        pltpu.make_async_copy(basis.at[slabs - 1], x_high, sems.at[2]),
        pltpu.make_async_copy(basis.at[:, pl.ds(0, 8)], y_low, sems.at[3]),
        pltpu.make_async_copy(basis.at[:, pl.ds(SLAB - 8, 8)], y_high, sems.at[4]),
    ]
    for copy in copies:
        copy.start()
    for copy in copies:
        copy.wait()

    def x_faces(low, high):
        low[0:SLAB, :] = x_low[...]
        high[0:SLAB, :] = x_high[...]
        first = jnp.zeros((SLAB, R), f32)
        last = jnp.zeros((SLAB, R), f32)
        for k in range(TERMS):
            rows = coef[k * SLAB : (k + 1) * SLAB, :]
            first = jnp.where(lane == k, rows[:, 0:1], first)
            last = jnp.where(lane == k, rows[:, slabs - 1 : slabs], last)
        low[SLAB : 2 * SLAB, :] = first
        high[SLAB : 2 * SLAB, :] = last

    def y_faces(low, high):
        for x in range(slabs):
            low[4 * x : 4 * x + 4, :] = y_low[x, 0:4, :]
            high[4 * x : 4 * x + 4, :] = y_high[x, 4:8, :]
        low[4 * slabs :, :] = jnp.zeros((16, R), f32)
        high[4 * slabs :, :] = jnp.zeros((16, R), f32)
        for k in range(TERMS):
            low[4 * (slabs + k) : 4 * (slabs + k) + 4, 0:slabs] = coef[k * SLAB : k * SLAB + 4, :]
            high[4 * (slabs + k) : 4 * (slabs + k) + 4, 0:slabs] = coef[(k + 1) * SLAB - 4 : (k + 1) * SLAB, :]

    pl.when(me[1] == 0)(lambda: x_faces(x_second, x_first))
    pl.when(me[1] != 0)(lambda: x_faces(x_first, x_second))
    pl.when(me[0] == 0)(lambda: y_faces(y_second, y_first))
    pl.when(me[0] != 0)(lambda: y_faces(y_first, y_second))


def turn_kernel(basis, turned):
    groups = turned.shape[0]
    for j in range(groups):
        one = basis[j * SLAB : (j + 1) * SLAB, :]
        two = basis[(j + groups) * SLAB : (j + groups + 1) * SLAB, :]
        turned[j] = jnp.concatenate([one, two], axis=0).T


def images_kernel(
    me, nominal_weights, turned, before, after, coef, x_first, x_second, y_first, y_second, mine, other, nominal,
    from_left, from_right, from_below, from_above, ends, above, below, face, top, bottom, product, squares, total,
):
    groups = turned.shape[0]
    slabs = 2 * groups

    def copied(*pairs):
        for source, target in pairs:
            target[...] = source[...]

    pl.when(me[1] == 0)(lambda: copied((x_second, from_left), (x_first, from_right)))
    pl.when(me[1] != 0)(lambda: copied((x_first, from_left), (x_second, from_right)))
    pl.when(me[0] == 0)(lambda: copied((y_second, from_below), (y_first, from_above)))
    pl.when(me[0] != 0)(lambda: copied((y_first, from_below), (y_second, from_above)))

    ends[0] = jnp.concatenate([from_left[0:SLAB, :], before[...]], axis=0).T
    ends[1] = jnp.concatenate([after[...], from_right[0:SLAB, :]], axis=0).T

    def strip(j, rows):
        if j < 0:
            return ends[0, rows, :]
        if j == groups:
            return ends[1, rows, :]
        return turned[j, rows, :]

    above[...] = from_above[0 : 4 * slabs, :].T
    below[...] = from_below[0 : 4 * slabs, :].T

    spot = lax.broadcasted_iota(jnp.int32, (groups, R), 1) % SLAB
    first = lax.broadcasted_iota(jnp.int32, (groups, R), 1) < SLAB
    group = lax.broadcasted_iota(jnp.int32, (groups, R), 0)
    level = spot % 4

    def joined(rows):
        return jnp.where(first, rows[0:groups], pltpu.roll(rows[groups:slabs], SLAB, 1))

    def flipped(tile):
        return jnp.concatenate([tile, jnp.zeros((R - tile.shape[0], R), f32)], axis=0).T

    left_coef = flipped(from_left[SLAB : 2 * SLAB, :])
    right_coef = flipped(from_right[SLAB : 2 * SLAB, :])
    above_coef = flipped(from_above[4 * slabs :, :])
    below_coef = flipped(from_below[4 * slabs :, :])
    for k in range(TERMS):
        rows = jnp.concatenate([coef[k * SLAB : (k + 1) * SLAB, :], jnp.zeros((SLAB, R - slabs), f32)], axis=1)
        own = joined(flipped(rows))
        half = pltpu.roll(own, SLAB, 1)
        left = jnp.where(first, left_coef[k : k + 1, :], half[groups - 1 : groups, :])
        left = jnp.where(group == 0, left, pltpu.roll(own, 1, 0))
        right = jnp.where(first, half[0:1, :], pltpu.roll(right_coef[k : k + 1, :], SLAB, 1))
        right = jnp.where(group == groups - 1, right, pltpu.roll(own, groups - 1, 0))
        up = jnp.where(
            spot < SLAB - 4,
            pltpu.roll(own, R - 4, 1),
            joined(pltpu.roll(above_coef, SLAB - 4 - 4 * k, 1)),
        )
        down = jnp.where(spot < 4, joined(pltpu.roll(below_coef, (R - 4 * k) % R, 1)), pltpu.roll(own, 4, 1))
        face[0, k] = 0.5 * (own + left)
        face[1, k] = 0.5 * (own + right)
        face[2, k] = 0.5 * (own + up)
        face[3, k] = 0.5 * (own + down)
        face[4, k] = 0.5 * (own + jnp.where(level < 3, pltpu.roll(own, R - 1, 1), 0.0))
        face[5, k] = 0.5 * (own + jnp.where(level > 0, pltpu.roll(own, 1, 1), 0.0))

    squares[...] = jnp.zeros_like(squares)
    lane = lax.broadcasted_iota(jnp.int32, (BLOCK, R), 1)
    inside = lane % SLAB
    depth = lane % 4

    def images(chunk, slot):
        for s in range(STEP):
            j = STEP * chunk + s
            weights = [[face[f, k, j : j + 1, :] for f in range(6)] for k in range(TERMS)]
            for start in range(0, R, BLOCK):
                rows = slice(start, start + BLOCK)
                v = turned[j, rows, :]
                up = pltpu.roll(above[rows, :], (SLAB - 4 - 4 * j) % R, 1)
                down = pltpu.roll(below[rows, :], (R - 4 * j) % R, 1)
                steps = (
                    v - strip(j - 1, rows),
                    v - strip(j + 1, rows),
                    v - jnp.where(inside < SLAB - 4, pltpu.roll(v, R - 4, 1), up),
                    v - jnp.where(inside < 4, down, pltpu.roll(v, 4, 1)),
                    v - jnp.where(depth < 3, pltpu.roll(v, R - 1, 1), 0.0),
                    v - jnp.where(depth > 0, pltpu.roll(v, 1, 1), 0.0),
                )
                summed_images = None
                for block in range(TERMS + 1):
                    if block == 0:
                        value = v
                    else:
                        k = block - 1
                        value = weights[k][0] * steps[0]
                        for weight, step in zip(weights[k][1:], steps[1:]):
                            value = value + weight * step
                        part = nominal_weights[k] * value
                        summed_images = part if summed_images is None else summed_images + part
                    high = value.astype(bf16)
                    rest = value - high.astype(f32)
                    squares[block, rows, :] += rest * rest
                    out = slice(block * R + start, block * R + start + BLOCK)
                    top[slot, out, s * R : (s + 1) * R] = high
                    bottom[slot, out, s * R : (s + 1) * R] = rest.astype(bf16)
                total[rows, :] = summed_images
            back = total[...].T
            nominal[j * SLAB : (j + 1) * SLAB, :] = back[0:SLAB]
            nominal[(j + groups) * SLAB : (j + groups + 1) * SLAB, :] = back[SLAB:]

    def grams(chunk, slot):
        for start in range(0, 2 * WIDTH, 256):
            rows = min(start + 256, WIDTH)
            if start + 256 <= WIDTH:
                right = top[slot, start : start + 256, :]
            elif start < WIDTH:
                right = jnp.concatenate([top[slot, start:WIDTH, :], bottom[slot, 0 : start + 256 - WIDTH, :]], axis=0)
            else:
                right = bottom[slot, start - WIDTH : start + 256 - WIDTH, :]
            value = lax.dot_general(
                top[slot, 0:rows, :], right, (((1,), (1,)), ((), ())), preferred_element_type=f32
            )
            if chunk == 0:
                product[0:rows, start : start + 256] = value
            else:
                product[0:rows, start : start + 256] += value

    chunks = groups // STEP
    for chunk in range(chunks):
        images(chunk, chunk % 2)
        if chunk > 0:
            grams(chunk - 1, (chunk - 1) % 2)
    grams(chunks - 1, (chunks - 1) % 2)

    r = lax.broadcasted_iota(jnp.int32, (R, R), 0)
    c = lax.broadcasted_iota(jnp.int32, (R, R), 1)

    def gram(a, b):
        high = product[a * R : (a + 1) * R, b * R : (b + 1) * R]
        one = product[a * R : (a + 1) * R, WIDTH + b * R : WIDTH + (b + 1) * R]
        two = product[b * R : (b + 1) * R, WIDTH + a * R : WIDTH + (a + 1) * R]
        if a != b:
            return high + one, two
        return high + one + jnp.where(r == c, jnp.sum(squares[a], axis=1, keepdims=True), 0.0), two

    def symmetric(a, b):
        one, two = gram(a, b)
        return one + two.T

    def diagonal(matrix):
        return jnp.sum(jnp.where(c == r, matrix, 0.0), axis=0, keepdims=True)

    base = symmetric(0, 0)
    for h, (even, full) in enumerate(halves):
        zero, one, two, three = [symmetric(*pair) for pair in even]
        tiles = [jnp.where(c >= r, base, zero), jnp.where(c >= r, one, two), jnp.where(c >= r, three, 0.0)]
        lines = []
        for line in (diagonal(zero), diagonal(two)):
            lines += [line, pltpu.roll(line, SLAB, 1)]
        for q, line in enumerate(lines):
            tiles[2] = jnp.where((r == R - 1 - q) & (c < SLAB), line, tiles[2])
        for pair in full:
            high, low = gram(*pair)
            tiles.append(high.T + low)

        def store(target, tiles=tiles):
            for q, tile in enumerate(tiles):
                target[q * R : (q + 1) * R, :] = tile

        pl.when(me[0] == h)(lambda: store(mine))
        pl.when(me[0] != h)(lambda: store(other))


def spread(value):
    return jnp.broadcast_to(value, (8, R))


def stacked(values, row8):
    out = values[-1]
    for i in range(len(values) - 2, -1, -1):
        out = jnp.where(row8 == i, values[i], out)
    return out


def panel_factor(rows, start):
    column = [spread(rows[:, start + l : start + l + 1]) for l in range(8)]
    a = [[spread(column[l][i : i + 1, :]) for l in range(i + 1)] for i in range(8)]
    inverse_pivot = [None] * 8
    lower = [[None] * 8 for _ in range(8)]
    for j in range(8):
        inverse_pivot[j] = 1.0 / a[j][j]
        for i in range(j + 1, 8):
            lower[i][j] = a[i][j] * inverse_pivot[j]
        for i in range(j + 1, 8):
            for l in range(j + 1, i + 1):
                a[i][l] = a[i][l] - lower[i][j] * a[l][j]
    turn = [[None] * 8 for _ in range(8)]
    for j in range(8):
        for i in range(j + 1, 8):
            value = lower[i][j]
            for l in range(j + 1, i):
                value = value + lower[i][l] * turn[l][j]
            turn[i][j] = -value
    return [a[j][j] for j in range(8)], inverse_pivot, turn


def factor_kernel(slot, inverse_t, inverse, *, cells):
    r = lax.broadcasted_iota(jnp.int32, (R, R), 0)
    c = lax.broadcasted_iota(jnp.int32, (R, R), 1)
    gram = jnp.where(c >= r, slot[...], slot[...].T) * (1.0 / cells)
    row8 = lax.broadcasted_iota(jnp.int32, (8, R), 0)
    lane8 = lax.broadcasted_iota(jnp.int32, (8, R), 1)
    panels = R // 8
    left = [gram[8 * i : 8 * i + 8, :] for i in range(panels)]
    right = [jnp.where(row8 + 8 * i == lane8, 1.0, 0.0).astype(f32) for i in range(panels)]
    for p in range(panels):
        start = 8 * p
        pivots, inverse_pivots, turn = panel_factor(left[p], start)
        ends = []
        for rows in (left[p], right[p]):
            out = rows
            for l in range(7):
                weight = jnp.where(row8 > l, turn[7][l], 0.0)
                for i in range(l + 1, 7):
                    weight = jnp.where(row8 == i, turn[i][l], weight)
                out = out + weight * spread(rows[l : l + 1, :])
            ends.append(out)
        inverse[start : start + 8, :] = ends[1] * stacked([1.0 / jnp.sqrt(pivot) for pivot in pivots], row8)
        if p == panels - 1:
            break
        scale = stacked(inverse_pivots, row8)
        solved = []
        for rows in ends:
            rows = rows * scale
            out = rows
            for i in range(1, 8):
                weight = jnp.where(row8 == 0, turn[i][0], 0.0)
                for l in range(1, i):
                    weight = jnp.where(row8 == l, turn[i][l], weight)
                out = out + weight * spread(rows[i : i + 1, :])
            solved.append(out)
        weights = [spread(left[p + 1][:, start + l : start + l + 1]) for l in range(8)]
        rest = left[p + 2 :]
        updates = []
        for out in solved:
            terms = [weights[l] * spread(out[l : l + 1, :]) for l in range(8)]
            while len(terms) > 1:
                terms = [terms[i] + terms[i + 1] for i in range(0, len(terms), 2)]
            updates.append(terms[0])
        left[p + 1] = left[p + 1] - updates[0]
        right[p + 1] = right[p + 1] - updates[1]
        if rest:
            columns = jnp.concatenate(rest, axis=0)[:, start : start + 8]
            update = jnp.dot(columns, jnp.concatenate(solved, axis=1), precision=HIGHEST, preferred_element_type=f32)
            for i in range(p + 2, panels):
                q = 8 * (i - p - 2)
                left[i] = left[i] - update[q : q + 8, :R]
                right[i] = right[i] - update[q : q + 8, R:]
    inverse_t[...] = inverse[...].T


def parts(value, count):
    out = []
    for _ in range(count):
        out.append(value.astype(bf16))
        value = value - out[-1].astype(f32)
    return out


def finish_kernel(
    me, mine, other, basis, nominal, inverse_t, ortho_hbm, nominal_hbm, reduced_hbm, residual_hbm,
    packed, ortho_out, nominal_out, reduced_out, residual_out, stage, sems, *, cells
):
    packed[pl.ds(pl.multiple_of(me[0] * HALF, R), HALF), :] = mine[...]
    packed[pl.ds(pl.multiple_of((1 - me[0]) * HALF, R), HALF), :] = other[...]
    high, middle, low = parts(inverse_t[...], 3)
    line = jnp.concatenate([high, middle], axis=1)
    square = jnp.concatenate([line, line], axis=0)
    last = jnp.concatenate([high, low], axis=0)

    def short(value):
        one, two = parts(value, 2)
        out = jnp.dot(jnp.concatenate([one, two], axis=1), square, preferred_element_type=f32)
        return out[:, :R] + out[:, R:]

    def product(value):
        one, two, three = parts(value, 3)
        out = jnp.dot(jnp.concatenate([one, two], axis=1), square, preferred_element_type=f32)
        end = jnp.dot(jnp.concatenate([three, one], axis=1), last, preferred_element_type=f32)
        return out[:, :R] + (out[:, R:] + end)

    copies = []

    def send(source, target):
        copies.append(pltpu.make_async_copy(source, target, sems.at[len(copies)]))
        copies[-1].start()

    step = 512
    for source, target, away in ((basis, ortho_out, ortho_hbm), (nominal, nominal_out, nominal_hbm)):
        for start in range(0, basis.shape[0], step):
            target[start : start + step, :] = short(source[start : start + step, :])
        send(target, away)

    r = lax.broadcasted_iota(jnp.int32, (R, R), 0)
    c = lax.broadcasted_iota(jnp.int32, (R, R), 1)
    scale = 1.0 / cells
    places = []
    for h, (even, full) in enumerate(halves):
        tiles = [packed[h * HALF + q * R : h * HALF + (q + 1) * R, :] for q in range(HALF_SLOTS)]
        turned = [tile.T for tile in tiles[:3]]
        lines = []
        for q in range(2):
            one = tiles[2][R - 1 - 2 * q : R - 2 * q, :]
            two = pltpu.roll(tiles[2][R - 2 - 2 * q : R - 1 - 2 * q, :], SLAB, 1)
            lines.append(jnp.where(c[0:1] < SLAB, one, two))
        matrices = [
            jnp.where(c < r, tiles[0], jnp.where(c == r, lines[0], turned[0])),
            jnp.where(c >= r, tiles[1], turned[1]),
            jnp.where(c < r, tiles[1], jnp.where(c == r, lines[1], turned[1])),
            jnp.where(c >= r, tiles[2], turned[2]),
        ] + tiles[3:]
        for (a, b), matrix in zip(even + full, matrices):
            at = len(places) * R
            stage[at : at + R, :] = matrix * scale
            places.append((reduced_out, b - 1) if a == 0 else (residual_out, operator_pairs.index((a - 1, b - 1))))
    moved = product(stage[...])
    for at in range(len(places)):
        stage[at * R : (at + 1) * R, :] = moved[at * R : (at + 1) * R, :].T
    moved = product(stage[...])
    for at, (target, index) in enumerate(places):
        target[index] = moved[at * R : (at + 1) * R, :]
    send(reduced_out, reduced_hbm)
    send(residual_out, residual_hbm)
    for copy in copies:
        copy.wait()


def summed(values, groups):
    count = lax.axis_size("gx")
    width = values.shape[1]
    parts = values.reshape(count, -1, width)
    shard = jnp.sum(lax.all_to_all(parts, "gx", 0, 0), axis=0)
    depth = len(groups[0])
    along = jnp.broadcast_to(shard[None], (depth,) + shard.shape)
    shard = jnp.sum(lax.all_to_all(along, "gy", 0, 0, axis_index_groups=groups), axis=0)
    spread = jnp.broadcast_to(shard[None], (count,) + shard.shape)
    return lax.all_to_all(spread, "gx", 0, 0).reshape(values.shape)


def shards(raw_basis, coefficients, nominal_weights):
    nx, ny, nz, width = raw_basis.shape
    count_x, count_y = lax.axis_size("gx"), lax.axis_size("gy")
    cells = nx * ny * nz * count_x * count_y
    flat = raw_basis.reshape(-1, width)
    coef = jnp.transpose(coefficients, (0, 2, 3, 1)).reshape(-1, nx)
    vmem = pl.BlockSpec(memory_space=pltpu.VMEM)
    smem = pl.BlockSpec(memory_space=pltpu.SMEM)
    hbm = pl.BlockSpec(memory_space=pltpu.HBM)

    def array(*shape):
        return jax.ShapeDtypeStruct(shape, f32)

    me = jnp.stack([lax.axis_index("gy") % 2, lax.axis_index("gx") % 2]).astype(jnp.int32)
    small = pltpu.CompilerParams(vmem_limit_bytes=VMEM_LIMIT)
    y_rows = 4 * nx + 4 * TERMS
    faces = pl.pallas_call(
        faces_kernel,
        out_shape=(array(2 * SLAB, R), array(2 * SLAB, R), array(y_rows, R), array(y_rows, R)),
        in_specs=[smem, hbm, hbm],
        out_specs=(vmem,) * 4,
        scratch_shapes=[
            pltpu.VMEM((SLAB, R), f32),
            pltpu.VMEM((SLAB, R), f32),
            pltpu.VMEM((nx, 8, R), f32),
            pltpu.VMEM((nx, 8, R), f32),
            pltpu.VMEM(coef.shape, f32),
            pltpu.SemaphoreType.DMA((5,)),
        ],
        compiler_params=small,
        name="faces",
    )(
        me,
        pltpu.with_memory_space_constraint(flat.reshape(nx, SLAB, width), pltpu.HBM),
        pltpu.with_memory_space_constraint(coef, pltpu.HBM),
    )

    def swaps(first, count):
        pairs = [(i, i + 1) for i in range(first, count - 1, 2)]
        return pairs + [(b, a) for a, b in pairs]

    halos = [
        lax.ppermute(face, axis, swaps(first, count))
        for face, axis, first, count in zip(faces, ("gx", "gx", "gy", "gy"), (0, 1, 0, 1), (count_x, count_x, count_y, count_y))
    ]
    groups = nx // 2
    turned = pl.pallas_call(
        turn_kernel,
        out_shape=array(groups, R, R),
        in_specs=[vmem],
        out_specs=vmem,
        compiler_params=small,
        name="turn",
    )(flat)

    mine, other, raw_nominal = pl.pallas_call(
        images_kernel,
        out_shape=(array(HALF, R), array(HALF, R), array(nx * SLAB, R)),
        grid=(1,),
        in_specs=[smem, smem, vmem]
        + [pl.BlockSpec((SLAB, R), lambda i, at=at: (at, 0)) for at in (groups - 1, groups)]
        + [vmem] * 5,
        out_specs=(vmem,) * 3,
        scratch_shapes=[
            pltpu.VMEM((2 * SLAB, R), f32),
            pltpu.VMEM((2 * SLAB, R), f32),
            pltpu.VMEM((y_rows, R), f32),
            pltpu.VMEM((y_rows, R), f32),
            pltpu.VMEM((2, R, R), f32),
            pltpu.VMEM((R, 4 * nx), f32),
            pltpu.VMEM((R, 4 * nx), f32),
            pltpu.VMEM((6, TERMS, groups, R), f32),
            pltpu.VMEM((2, WIDTH, STEP * R), bf16),
            pltpu.VMEM((2, WIDTH, STEP * R), bf16),
            pltpu.VMEM((WIDTH, 2 * WIDTH), f32),
            pltpu.VMEM((TERMS + 1, R, R), f32),
            pltpu.VMEM((R, R), f32),
        ],
        compiler_params=small,
        name="images",
    )(me, nominal_weights, turned, flat, flat, coef, *halos)

    swap = [(i, i ^ 1) for i in range(count_y)]
    along_z = [list(range(core, count_y, 2)) for core in range(2)]
    mine = mine + lax.ppermute(other, "gy", swap)
    mine = summed(mine, along_z)
    other = lax.ppermute(mine, "gy", swap)

    def factor(*refs):
        factor_kernel(*refs, cells=cells)

    def finish(*refs):
        finish_kernel(*refs, cells=cells)

    inverse_t = pl.pallas_call(
        factor,
        out_shape=array(R, R),
        grid=(1,),
        in_specs=[pl.BlockSpec((R, R), lambda i: (0, 0))],
        out_specs=pl.BlockSpec((R, R), lambda i: (0, 0)),
        scratch_shapes=[pltpu.VMEM((R, R), f32)],
        compiler_params=small,
        name="factor",
    )(mine)
    ortho, nominal, reduced_ops, residual_grams = pl.pallas_call(
        finish,
        out_shape=(array(nx * SLAB, R), array(nx * SLAB, R), array(TERMS, R, R), array(len(operator_pairs), R, R)),
        in_specs=[smem] + [vmem] * 5,
        out_specs=(hbm,) * 4,
        scratch_shapes=[
            pltpu.VMEM((2 * HALF, R), f32),
            pltpu.VMEM((nx * SLAB, R), f32),
            pltpu.VMEM((nx * SLAB, R), f32),
            pltpu.VMEM((TERMS, R, R), f32),
            pltpu.VMEM((len(operator_pairs), R, R), f32),
            pltpu.VMEM(((TERMS + len(operator_pairs)) * R, R), f32),
            pltpu.SemaphoreType.DMA((4,)),
        ],
        compiler_params=small,
        name="finish",
    )(me, mine, other, flat, raw_nominal, inverse_t)
    shape = raw_basis.shape
    return (ortho.reshape(shape), nominal.reshape(shape), reduced_ops, residual_grams)


def solution(mesh):
    in_specs = (P("gx", "gy", None, None), P(None, "gx", "gy", None), P())
    out_specs = (P("gx", "gy", None, None), P("gx", "gy", None, None), P(), P())
    return jax.shard_map(shards, mesh=mesh, in_specs=in_specs, out_specs=out_specs, check_vma=False)
```

```python
import jax
import jax.numpy as jnp
from jax import lax
from jax.experimental import pallas as pl
from jax.experimental.pallas import tpu as pltpu
from jax.sharding import PartitionSpec as P

R = 128
TERMS = 4
operator_pairs = ((0, 0), (0, 1), (0, 2), (0, 3), (1, 1), (1, 2), (1, 3), (2, 2), (2, 3), (3, 3))
crossed_pairs = tuple(pair for pair in operator_pairs if pair[0] != pair[1])
HIGHEST = lax.Precision.HIGHEST
f32, bf16 = jnp.float32, jnp.bfloat16

HALF_SLOTS = 6
HALF = HALF_SLOTS * R
SLAB = 64
WIDTH = (TERMS + 1) * R
BLOCK = 32
STEP = 4
VMEM_LIMIT = 24 * 2**20
halves = (
    ([(0, k + 1) for k in range(TERMS)], [(a + 1, b + 1) for a, b in crossed_pairs[:3]]),
    ([(k + 1, k + 1) for k in range(TERMS)], [(a + 1, b + 1) for a, b in crossed_pairs[3:]]),
)


def faces_kernel(me, basis, coef_in, x_first, x_second, y_first, y_second, x_low, x_high, y_low, y_high, coef, sems):
    lane = lax.broadcasted_iota(jnp.int32, (SLAB, R), 1)
    slabs = basis.shape[0]
    copies = [
        pltpu.make_async_copy(coef_in, coef, sems.at[0]),
        pltpu.make_async_copy(basis.at[0], x_low, sems.at[1]),
        pltpu.make_async_copy(basis.at[slabs - 1], x_high, sems.at[2]),
        pltpu.make_async_copy(basis.at[:, pl.ds(0, 8)], y_low, sems.at[3]),
        pltpu.make_async_copy(basis.at[:, pl.ds(SLAB - 8, 8)], y_high, sems.at[4]),
    ]
    for copy in copies:
        copy.start()
    for copy in copies:
        copy.wait()

    def x_faces(low, high):
        low[0:SLAB, :] = x_low[...]
        high[0:SLAB, :] = x_high[...]
        first = jnp.zeros((SLAB, R), f32)
        last = jnp.zeros((SLAB, R), f32)
        for k in range(TERMS):
            rows = coef[k * SLAB : (k + 1) * SLAB, :]
            first = jnp.where(lane == k, rows[:, 0:1], first)
            last = jnp.where(lane == k, rows[:, slabs - 1 : slabs], last)
        low[SLAB : 2 * SLAB, :] = first
        high[SLAB : 2 * SLAB, :] = last

    def y_faces(low, high):
        for x in range(slabs):
            low[4 * x : 4 * x + 4, :] = y_low[x, 0:4, :]
            high[4 * x : 4 * x + 4, :] = y_high[x, 4:8, :]
        low[4 * slabs :, :] = jnp.zeros((16, R), f32)
        high[4 * slabs :, :] = jnp.zeros((16, R), f32)
        for k in range(TERMS):
            low[4 * (slabs + k) : 4 * (slabs + k) + 4, 0:slabs] = coef[k * SLAB : k * SLAB + 4, :]
            high[4 * (slabs + k) : 4 * (slabs + k) + 4, 0:slabs] = coef[(k + 1) * SLAB - 4 : (k + 1) * SLAB, :]

    pl.when(me[1] == 0)(lambda: x_faces(x_second, x_first))
    pl.when(me[1] != 0)(lambda: x_faces(x_first, x_second))
    pl.when(me[0] == 0)(lambda: y_faces(y_second, y_first))
    pl.when(me[0] != 0)(lambda: y_faces(y_first, y_second))


def turn_kernel(basis, turned):
    groups = turned.shape[0]
    for j in range(groups):
        one = basis[j * SLAB : (j + 1) * SLAB, :]
        two = basis[(j + groups) * SLAB : (j + groups + 1) * SLAB, :]
        turned[j] = jnp.concatenate([one, two], axis=0).T


def images_kernel(
    me, nominal_weights, turned, before, after, coef, x_first, x_second, y_first, y_second, mine, other, nominal,
    from_left, from_right, from_below, from_above, ends, above, below, face, top, bottom, product, squares, total,
):
    groups = turned.shape[0]
    slabs = 2 * groups

    def copied(*pairs):
        for source, target in pairs:
            target[...] = source[...]

    pl.when(me[1] == 0)(lambda: copied((x_second, from_left), (x_first, from_right)))
    pl.when(me[1] != 0)(lambda: copied((x_first, from_left), (x_second, from_right)))
    pl.when(me[0] == 0)(lambda: copied((y_second, from_below), (y_first, from_above)))
    pl.when(me[0] != 0)(lambda: copied((y_first, from_below), (y_second, from_above)))

    ends[0] = jnp.concatenate([from_left[0:SLAB, :], before[...]], axis=0).T
    ends[1] = jnp.concatenate([after[...], from_right[0:SLAB, :]], axis=0).T

    def strip(j, rows):
        if j < 0:
            return ends[0, rows, :]
        if j == groups:
            return ends[1, rows, :]
        return turned[j, rows, :]

    above[...] = from_above[0 : 4 * slabs, :].T
    below[...] = from_below[0 : 4 * slabs, :].T

    spot = lax.broadcasted_iota(jnp.int32, (groups, R), 1) % SLAB
    first = lax.broadcasted_iota(jnp.int32, (groups, R), 1) < SLAB
    group = lax.broadcasted_iota(jnp.int32, (groups, R), 0)
    level = spot % 4

    def joined(rows):
        return jnp.where(first, rows[0:groups], pltpu.roll(rows[groups:slabs], SLAB, 1))

    def flipped(tile):
        return jnp.concatenate([tile, jnp.zeros((R - tile.shape[0], R), f32)], axis=0).T

    left_coef = flipped(from_left[SLAB : 2 * SLAB, :])
    right_coef = flipped(from_right[SLAB : 2 * SLAB, :])
    above_coef = flipped(from_above[4 * slabs :, :])
    below_coef = flipped(from_below[4 * slabs :, :])
    for k in range(TERMS):
        rows = jnp.concatenate([coef[k * SLAB : (k + 1) * SLAB, :], jnp.zeros((SLAB, R - slabs), f32)], axis=1)
        own = joined(flipped(rows))
        half = pltpu.roll(own, SLAB, 1)
        left = jnp.where(first, left_coef[k : k + 1, :], half[groups - 1 : groups, :])
        left = jnp.where(group == 0, left, pltpu.roll(own, 1, 0))
        right = jnp.where(first, half[0:1, :], pltpu.roll(right_coef[k : k + 1, :], SLAB, 1))
        right = jnp.where(group == groups - 1, right, pltpu.roll(own, groups - 1, 0))
        up = jnp.where(
            spot < SLAB - 4,
            pltpu.roll(own, R - 4, 1),
            joined(pltpu.roll(above_coef, SLAB - 4 - 4 * k, 1)),
        )
        down = jnp.where(spot < 4, joined(pltpu.roll(below_coef, (R - 4 * k) % R, 1)), pltpu.roll(own, 4, 1))
        face[0, k] = 0.5 * (own + left)
        face[1, k] = 0.5 * (own + right)
        face[2, k] = 0.5 * (own + up)
        face[3, k] = 0.5 * (own + down)
        face[4, k] = 0.5 * (own + jnp.where(level < 3, pltpu.roll(own, R - 1, 1), 0.0))
        face[5, k] = 0.5 * (own + jnp.where(level > 0, pltpu.roll(own, 1, 1), 0.0))

    squares[...] = jnp.zeros_like(squares)
    lane = lax.broadcasted_iota(jnp.int32, (BLOCK, R), 1)
    inside = lane % SLAB
    depth = lane % 4

    def images(chunk, slot):
        for s in range(STEP):
            j = STEP * chunk + s
            weights = [[face[f, k, j : j + 1, :] for f in range(6)] for k in range(TERMS)]
            for start in range(0, R, BLOCK):
                rows = slice(start, start + BLOCK)
                v = turned[j, rows, :]
                up = pltpu.roll(above[rows, :], (SLAB - 4 - 4 * j) % R, 1)
                down = pltpu.roll(below[rows, :], (R - 4 * j) % R, 1)
                steps = (
                    v - strip(j - 1, rows),
                    v - strip(j + 1, rows),
                    v - jnp.where(inside < SLAB - 4, pltpu.roll(v, R - 4, 1), up),
                    v - jnp.where(inside < 4, down, pltpu.roll(v, 4, 1)),
                    v - jnp.where(depth < 3, pltpu.roll(v, R - 1, 1), 0.0),
                    v - jnp.where(depth > 0, pltpu.roll(v, 1, 1), 0.0),
                )
                summed_images = None
                for block in range(TERMS + 1):
                    if block == 0:
                        value = v
                    else:
                        k = block - 1
                        value = weights[k][0] * steps[0]
                        for weight, step in zip(weights[k][1:], steps[1:]):
                            value = value + weight * step
                        part = nominal_weights[k] * value
                        summed_images = part if summed_images is None else summed_images + part
                    high = value.astype(bf16)
                    rest = value - high.astype(f32)
                    squares[block, rows, :] += rest * rest
                    out = slice(block * R + start, block * R + start + BLOCK)
                    top[slot, out, s * R : (s + 1) * R] = high
                    bottom[slot, out, s * R : (s + 1) * R] = rest.astype(bf16)
                total[rows, :] = summed_images
            back = total[...].T
            nominal[j * SLAB : (j + 1) * SLAB, :] = back[0:SLAB]
            nominal[(j + groups) * SLAB : (j + groups + 1) * SLAB, :] = back[SLAB:]

    def grams(chunk, slot):
        for start in range(0, 2 * WIDTH, 256):
            rows = min(start + 256, WIDTH)
            if start + 256 <= WIDTH:
                right = top[slot, start : start + 256, :]
            elif start < WIDTH:
                right = jnp.concatenate([top[slot, start:WIDTH, :], bottom[slot, 0 : start + 256 - WIDTH, :]], axis=0)
            else:
                right = bottom[slot, start - WIDTH : start + 256 - WIDTH, :]
            value = lax.dot_general(
                top[slot, 0:rows, :], right, (((1,), (1,)), ((), ())), preferred_element_type=f32
            )
            if chunk == 0:
                product[0:rows, start : start + 256] = value
            else:
                product[0:rows, start : start + 256] += value

    chunks = groups // STEP
    for chunk in range(chunks):
        images(chunk, chunk % 2)
        if chunk > 0:
            grams(chunk - 1, (chunk - 1) % 2)
    grams(chunks - 1, (chunks - 1) % 2)

    r = lax.broadcasted_iota(jnp.int32, (R, R), 0)
    c = lax.broadcasted_iota(jnp.int32, (R, R), 1)

    def gram(a, b):
        high = product[a * R : (a + 1) * R, b * R : (b + 1) * R]
        one = product[a * R : (a + 1) * R, WIDTH + b * R : WIDTH + (b + 1) * R]
        two = product[b * R : (b + 1) * R, WIDTH + a * R : WIDTH + (a + 1) * R]
        if a != b:
            return high + one, two
        return high + one + jnp.where(r == c, jnp.sum(squares[a], axis=1, keepdims=True), 0.0), two

    def symmetric(a, b):
        one, two = gram(a, b)
        return one + two.T

    def diagonal(matrix):
        return jnp.sum(jnp.where(c == r, matrix, 0.0), axis=0, keepdims=True)

    base = symmetric(0, 0)
    for h, (even, full) in enumerate(halves):
        zero, one, two, three = [symmetric(*pair) for pair in even]
        tiles = [jnp.where(c >= r, base, zero), jnp.where(c >= r, one, two), jnp.where(c >= r, three, 0.0)]
        lines = []
        for line in (diagonal(zero), diagonal(two)):
            lines += [line, pltpu.roll(line, SLAB, 1)]
        for q, line in enumerate(lines):
            tiles[2] = jnp.where((r == R - 1 - q) & (c < SLAB), line, tiles[2])
        for pair in full:
            high, low = gram(*pair)
            tiles.append(high.T + low)

        def store(target, tiles=tiles):
            for q, tile in enumerate(tiles):
                target[q * R : (q + 1) * R, :] = tile

        pl.when(me[0] == h)(lambda: store(mine))
        pl.when(me[0] != h)(lambda: store(other))


def spread(value):
    return jnp.broadcast_to(value, (8, R))


def stacked(values, row8):
    out = values[-1]
    for i in range(len(values) - 2, -1, -1):
        out = jnp.where(row8 == i, values[i], out)
    return out


def panel_factor(rows, start):
    column = [spread(rows[:, start + l : start + l + 1]) for l in range(8)]
    a = [[spread(column[l][i : i + 1, :]) for l in range(i + 1)] for i in range(8)]
    inverse_pivot = [None] * 8
    lower = [[None] * 8 for _ in range(8)]
    for j in range(8):
        inverse_pivot[j] = 1.0 / a[j][j]
        for i in range(j + 1, 8):
            lower[i][j] = a[i][j] * inverse_pivot[j]
        for i in range(j + 1, 8):
            for l in range(j + 1, i + 1):
                a[i][l] = a[i][l] - lower[i][j] * a[l][j]
    turn = [[None] * 8 for _ in range(8)]
    for j in range(8):
        for i in range(j + 1, 8):
            value = lower[i][j]
            for l in range(j + 1, i):
                value = value + lower[i][l] * turn[l][j]
            turn[i][j] = -value
    return [a[j][j] for j in range(8)], inverse_pivot, turn


def factor_kernel(slot, inverse_t, inverse, *, cells):
    r = lax.broadcasted_iota(jnp.int32, (R, R), 0)
    c = lax.broadcasted_iota(jnp.int32, (R, R), 1)
    gram = jnp.where(c >= r, slot[...], slot[...].T) * (1.0 / cells)
    row8 = lax.broadcasted_iota(jnp.int32, (8, R), 0)
    lane8 = lax.broadcasted_iota(jnp.int32, (8, R), 1)
    panels = R // 8
    left = [gram[8 * i : 8 * i + 8, :] for i in range(panels)]
    right = [jnp.where(row8 + 8 * i == lane8, 1.0, 0.0).astype(f32) for i in range(panels)]
    for p in range(panels):
        start = 8 * p
        pivots, inverse_pivots, turn = panel_factor(left[p], start)
        ends = []
        for rows in (left[p], right[p]):
            out = rows
            for l in range(7):
                weight = jnp.where(row8 > l, turn[7][l], 0.0)
                for i in range(l + 1, 7):
                    weight = jnp.where(row8 == i, turn[i][l], weight)
                out = out + weight * spread(rows[l : l + 1, :])
            ends.append(out)
        inverse[start : start + 8, :] = ends[1] * stacked([1.0 / jnp.sqrt(pivot) for pivot in pivots], row8)
        if p == panels - 1:
            break
        scale = stacked(inverse_pivots, row8)
        solved = []
        for rows in ends:
            rows = rows * scale
            out = rows
            for i in range(1, 8):
                weight = jnp.where(row8 == 0, turn[i][0], 0.0)
                for l in range(1, i):
                    weight = jnp.where(row8 == l, turn[i][l], weight)
                out = out + weight * spread(rows[i : i + 1, :])
            solved.append(out)
        weights = [spread(left[p + 1][:, start + l : start + l + 1]) for l in range(8)]
        rest = left[p + 2 :]
        updates = []
        for out in solved:
            terms = [weights[l] * spread(out[l : l + 1, :]) for l in range(8)]
            while len(terms) > 1:
                terms = [terms[i] + terms[i + 1] for i in range(0, len(terms), 2)]
            updates.append(terms[0])
        left[p + 1] = left[p + 1] - updates[0]
        right[p + 1] = right[p + 1] - updates[1]
        if rest:
            columns = jnp.concatenate(rest, axis=0)[:, start : start + 8]
            update = jnp.dot(columns, jnp.concatenate(solved, axis=1), precision=HIGHEST, preferred_element_type=f32)
            for i in range(p + 2, panels):
                q = 8 * (i - p - 2)
                left[i] = left[i] - update[q : q + 8, :R]
                right[i] = right[i] - update[q : q + 8, R:]
    inverse_t[...] = inverse[...].T


def parts(value, count):
    out = []
    for _ in range(count):
        out.append(value.astype(bf16))
        value = value - out[-1].astype(f32)
    return out


def finish_kernel(
    me, mine, other, basis, nominal, inverse_t, ortho_hbm, nominal_hbm, reduced_hbm, residual_hbm,
    packed, ortho_out, nominal_out, reduced_out, residual_out, stage, sems, *, cells
):
    packed[pl.ds(pl.multiple_of(me[0] * HALF, R), HALF), :] = mine[...]
    packed[pl.ds(pl.multiple_of((1 - me[0]) * HALF, R), HALF), :] = other[...]
    high, middle, low = parts(inverse_t[...], 3)
    line = jnp.concatenate([high, middle], axis=1)
    square = jnp.concatenate([line, line], axis=0)
    last = jnp.concatenate([high, low], axis=0)

    def short(value):
        one, two = parts(value, 2)
        out = jnp.dot(jnp.concatenate([one, two], axis=1), square, preferred_element_type=f32)
        return out[:, :R] + out[:, R:]

    def product(value):
        one, two, three = parts(value, 3)
        out = jnp.dot(jnp.concatenate([one, two], axis=1), square, preferred_element_type=f32)
        end = jnp.dot(jnp.concatenate([three, one], axis=1), last, preferred_element_type=f32)
        return out[:, :R] + (out[:, R:] + end)

    copies = []

    def send(source, target):
        copies.append(pltpu.make_async_copy(source, target, sems.at[len(copies)]))
        copies[-1].start()

    step = 512
    for source, target, away in ((basis, ortho_out, ortho_hbm), (nominal, nominal_out, nominal_hbm)):
        for start in range(0, basis.shape[0], step):
            target[start : start + step, :] = short(source[start : start + step, :])
        send(target, away)

    r = lax.broadcasted_iota(jnp.int32, (R, R), 0)
    c = lax.broadcasted_iota(jnp.int32, (R, R), 1)
    scale = 1.0 / cells
    places = []
    for h, (even, full) in enumerate(halves):
        tiles = [packed[h * HALF + q * R : h * HALF + (q + 1) * R, :] for q in range(HALF_SLOTS)]
        turned = [tile.T for tile in tiles[:3]]
        lines = []
        for q in range(2):
            one = tiles[2][R - 1 - 2 * q : R - 2 * q, :]
            two = pltpu.roll(tiles[2][R - 2 - 2 * q : R - 1 - 2 * q, :], SLAB, 1)
            lines.append(jnp.where(c[0:1] < SLAB, one, two))
        matrices = [
            jnp.where(c < r, tiles[0], jnp.where(c == r, lines[0], turned[0])),
            jnp.where(c >= r, tiles[1], turned[1]),
            jnp.where(c < r, tiles[1], jnp.where(c == r, lines[1], turned[1])),
            jnp.where(c >= r, tiles[2], turned[2]),
        ] + tiles[3:]
        for (a, b), matrix in zip(even + full, matrices):
            at = len(places) * R
            stage[at : at + R, :] = matrix * scale
            places.append((reduced_out, b - 1) if a == 0 else (residual_out, operator_pairs.index((a - 1, b - 1))))
    moved = product(stage[...])
    for at in range(len(places)):
        stage[at * R : (at + 1) * R, :] = moved[at * R : (at + 1) * R, :].T
    moved = product(stage[...])
    for at, (target, index) in enumerate(places):
        target[index] = moved[at * R : (at + 1) * R, :]
    send(reduced_out, reduced_hbm)
    send(residual_out, residual_hbm)
    for copy in copies:
        copy.wait()


def summed(values, groups):
    count = lax.axis_size("gx")
    width = values.shape[1]
    parts = values.reshape(count, -1, width)
    shard = jnp.sum(lax.all_to_all(parts, "gx", 0, 0), axis=0)
    depth = len(groups[0])
    along = jnp.broadcast_to(shard[None], (depth,) + shard.shape)
    shard = jnp.sum(lax.all_to_all(along, "gy", 0, 0, axis_index_groups=groups), axis=0)
    spread = jnp.broadcast_to(shard[None], (count,) + shard.shape)
    return lax.all_to_all(spread, "gx", 0, 0).reshape(values.shape)


def shards(raw_basis, coefficients, nominal_weights):
    nx, ny, nz, width = raw_basis.shape
    count_x, count_y = lax.axis_size("gx"), lax.axis_size("gy")
    cells = nx * ny * nz * count_x * count_y
    flat = raw_basis.reshape(-1, width)
    coef = jnp.transpose(coefficients, (0, 2, 3, 1)).reshape(-1, nx)
    vmem = pl.BlockSpec(memory_space=pltpu.VMEM)
    smem = pl.BlockSpec(memory_space=pltpu.SMEM)
    hbm = pl.BlockSpec(memory_space=pltpu.HBM)

    def array(*shape):
        return jax.ShapeDtypeStruct(shape, f32)

    me = jnp.stack([lax.axis_index("gy") % 2, lax.axis_index("gx") % 2]).astype(jnp.int32)
    small = pltpu.CompilerParams(vmem_limit_bytes=VMEM_LIMIT)
    y_rows = 4 * nx + 4 * TERMS
    faces = pl.pallas_call(
        faces_kernel,
        out_shape=(array(2 * SLAB, R), array(2 * SLAB, R), array(y_rows, R), array(y_rows, R)),
        in_specs=[smem, hbm, hbm],
        out_specs=(vmem,) * 4,
        scratch_shapes=[
            pltpu.VMEM((SLAB, R), f32),
            pltpu.VMEM((SLAB, R), f32),
            pltpu.VMEM((nx, 8, R), f32),
            pltpu.VMEM((nx, 8, R), f32),
            pltpu.VMEM(coef.shape, f32),
            pltpu.SemaphoreType.DMA((5,)),
        ],
        compiler_params=small,
        name="faces",
    )(
        me,
        pltpu.with_memory_space_constraint(flat.reshape(nx, SLAB, width), pltpu.HBM),
        pltpu.with_memory_space_constraint(coef, pltpu.HBM),
    )

    def swaps(first, count):
        pairs = [(i, i + 1) for i in range(first, count - 1, 2)]
        return pairs + [(b, a) for a, b in pairs]

    halos = []
    for face, axis, first in zip(faces, ("gx", "gx", "gy", "gy"), (0, 1, 0, 1)):
        halos.append(lax.ppermute(face, axis, swaps(first, lax.axis_size(axis))))
    groups = nx // 2
    turned = pl.pallas_call(
        turn_kernel,
        out_shape=array(groups, R, R),
        in_specs=[vmem],
        out_specs=vmem,
        compiler_params=small,
        name="turn",
    )(flat)

    mine, other, raw_nominal = pl.pallas_call(
        images_kernel,
        out_shape=(array(HALF, R), array(HALF, R), array(nx * SLAB, R)),
        grid=(1,),
        in_specs=[smem, smem, vmem]
        + [pl.BlockSpec((SLAB, R), lambda i, at=at: (at, 0)) for at in (groups - 1, groups)]
        + [vmem] * 5,
        out_specs=(vmem,) * 3,
        scratch_shapes=[
            pltpu.VMEM((2 * SLAB, R), f32),
            pltpu.VMEM((2 * SLAB, R), f32),
            pltpu.VMEM((y_rows, R), f32),
            pltpu.VMEM((y_rows, R), f32),
            pltpu.VMEM((2, R, R), f32),
            pltpu.VMEM((R, 4 * nx), f32),
            pltpu.VMEM((R, 4 * nx), f32),
            pltpu.VMEM((6, TERMS, groups, R), f32),
            pltpu.VMEM((2, WIDTH, STEP * R), bf16),
            pltpu.VMEM((2, WIDTH, STEP * R), bf16),
            pltpu.VMEM((WIDTH, 2 * WIDTH), f32),
            pltpu.VMEM((TERMS + 1, R, R), f32),
            pltpu.VMEM((R, R), f32),
        ],
        compiler_params=small,
        name="images",
    )(me, nominal_weights, turned, flat, flat, coef, *halos)

    swap = [(i, i ^ 1) for i in range(count_y)]
    along_z = [list(range(core, count_y, 2)) for core in range(2)]
    mine = mine + lax.ppermute(other, "gy", swap)
    mine = summed(mine, along_z)
    other = lax.ppermute(mine, "gy", swap)

    def factor(*refs):
        factor_kernel(*refs, cells=cells)

    def finish(*refs):
        finish_kernel(*refs, cells=cells)

    inverse_t = pl.pallas_call(
        factor,
        out_shape=array(R, R),
        grid=(1,),
        in_specs=[pl.BlockSpec((R, R), lambda i: (0, 0))],
        out_specs=pl.BlockSpec((R, R), lambda i: (0, 0)),
        scratch_shapes=[pltpu.VMEM((R, R), f32)],
        compiler_params=small,
        name="factor",
    )(mine)
    ortho, nominal, reduced_ops, residual_grams = pl.pallas_call(
        finish,
        out_shape=(array(nx * SLAB, R), array(nx * SLAB, R), array(TERMS, R, R), array(len(operator_pairs), R, R)),
        in_specs=[smem] + [vmem] * 5,
        out_specs=(hbm,) * 4,
        scratch_shapes=[
            pltpu.VMEM((2 * HALF, R), f32),
            pltpu.VMEM((nx * SLAB, R), f32),
            pltpu.VMEM((nx * SLAB, R), f32),
            pltpu.VMEM((TERMS, R, R), f32),
            pltpu.VMEM((len(operator_pairs), R, R), f32),
            pltpu.VMEM(((TERMS + len(operator_pairs)) * R, R), f32),
            pltpu.SemaphoreType.DMA((4,)),
        ],
        compiler_params=small,
        name="finish",
    )(me, mine, other, flat, raw_nominal, inverse_t)
    shape = raw_basis.shape
    return (ortho.reshape(shape), nominal.reshape(shape), reduced_ops, residual_grams)


def solution(mesh):
    in_specs = (P("gx", "gy", None, None), P(None, "gx", "gy", None), P())
    out_specs = (P("gx", "gy", None, None), P("gx", "gy", None, None), P(), P())
    return jax.shard_map(shards, mesh=mesh, in_specs=in_specs, out_specs=out_specs, check_vma=False)
```

```python
import jax
import jax.numpy as jnp
from jax import lax
from jax.experimental import pallas as pl
from jax.experimental.pallas import tpu as pltpu
from jax.sharding import PartitionSpec as P

R = 128
TERMS = 4
operator_pairs = ((0, 0), (0, 1), (0, 2), (0, 3), (1, 1), (1, 2), (1, 3), (2, 2), (2, 3), (3, 3))
crossed_pairs = tuple(pair for pair in operator_pairs if pair[0] != pair[1])
HIGHEST = lax.Precision.HIGHEST
f32, bf16 = jnp.float32, jnp.bfloat16

HALF_SLOTS = 6
HALF = HALF_SLOTS * R
SLAB = 64
WIDTH = (TERMS + 1) * R
BLOCK = 32
STEP = 4
VMEM_LIMIT = 24 * 2**20
halves = (
    ([(0, k + 1) for k in range(TERMS)], [(a + 1, b + 1) for a, b in crossed_pairs[:3]]),
    ([(k + 1, k + 1) for k in range(TERMS)], [(a + 1, b + 1) for a, b in crossed_pairs[3:]]),
)


def flipped(tile):
    return jnp.concatenate([tile, jnp.zeros((R - tile.shape[0], R), f32)], axis=0).T


def faces_kernel(me, basis, coef_in, x_first, x_second, y_first, y_second, x_low, x_high, y_low, y_high, coef, sems):
    lane = lax.broadcasted_iota(jnp.int32, (SLAB, R), 1)
    slabs = basis.shape[0]
    copies = [
        pltpu.make_async_copy(coef_in, coef, sems.at[0]),
        pltpu.make_async_copy(basis.at[0], x_low, sems.at[1]),
        pltpu.make_async_copy(basis.at[slabs - 1], x_high, sems.at[2]),
        pltpu.make_async_copy(basis.at[:, pl.ds(0, 8)], y_low, sems.at[3]),
        pltpu.make_async_copy(basis.at[:, pl.ds(SLAB - 8, 8)], y_high, sems.at[4]),
    ]
    for copy in copies:
        copy.start()
    for copy in copies:
        copy.wait()

    def x_faces(low, high):
        low[0:SLAB, :] = x_low[...]
        high[0:SLAB, :] = x_high[...]
        both = jnp.zeros((SLAB, R), f32)
        for k in range(TERMS):
            rows = coef[k * SLAB : (k + 1) * SLAB, :]
            both = jnp.where(lane == k, rows[:, 0:1], both)
            both = jnp.where(lane == k + TERMS, rows[:, slabs - 1 : slabs], both)
        lines = flipped(both)[0 : 2 * TERMS]
        low[SLAB:, :] = lines
        high[SLAB:, :] = lines

    def y_faces(low, high):
        for x in range(slabs):
            low[4 * x : 4 * x + 4, :] = y_low[x, 0:4, :]
            high[4 * x : 4 * x + 4, :] = y_high[x, 4:8, :]
        low[4 * slabs :, :] = jnp.zeros((16, R), f32)
        high[4 * slabs :, :] = jnp.zeros((16, R), f32)
        for k in range(TERMS):
            low[4 * (slabs + k) : 4 * (slabs + k) + 4, 0:slabs] = coef[k * SLAB : k * SLAB + 4, :]
            high[4 * (slabs + k) : 4 * (slabs + k) + 4, 0:slabs] = coef[(k + 1) * SLAB - 4 : (k + 1) * SLAB, :]

    pl.when(me[1] == 0)(lambda: x_faces(x_second, x_first))
    pl.when(me[1] != 0)(lambda: x_faces(x_first, x_second))
    pl.when(me[0] == 0)(lambda: y_faces(y_second, y_first))
    pl.when(me[0] != 0)(lambda: y_faces(y_first, y_second))


def turn_kernel(basis, turned):
    groups = turned.shape[0]
    for j in range(groups):
        one = basis[j * SLAB : (j + 1) * SLAB, :]
        two = basis[(j + groups) * SLAB : (j + groups + 1) * SLAB, :]
        turned[j] = jnp.concatenate([one, two], axis=0).T


def images_kernel(
    me, nominal_weights, turned, before, after, coef, x_first, x_second, y_first, y_second, mine, other, nominal,
    from_left, from_right, from_below, from_above, ends, above, below, face, top, bottom, product, squares, total,
):
    groups = turned.shape[0]
    slabs = 2 * groups

    def copied(*pairs):
        for source, target in pairs:
            target[...] = source[...]

    pl.when(me[1] == 0)(lambda: copied((x_second, from_left), (x_first, from_right)))
    pl.when(me[1] != 0)(lambda: copied((x_first, from_left), (x_second, from_right)))
    pl.when(me[0] == 0)(lambda: copied((y_second, from_below), (y_first, from_above)))
    pl.when(me[0] != 0)(lambda: copied((y_first, from_below), (y_second, from_above)))

    ends[0] = jnp.concatenate([from_left[0:SLAB, :], before[...]], axis=0).T
    ends[1] = jnp.concatenate([after[...], from_right[0:SLAB, :]], axis=0).T

    def strip(j, rows):
        if j < 0:
            return ends[0, rows, :]
        if j == groups:
            return ends[1, rows, :]
        return turned[j, rows, :]

    above[...] = from_above[0 : 4 * slabs, :].T
    below[...] = from_below[0 : 4 * slabs, :].T

    spot = lax.broadcasted_iota(jnp.int32, (groups, R), 1) % SLAB
    first = lax.broadcasted_iota(jnp.int32, (groups, R), 1) < SLAB
    group = lax.broadcasted_iota(jnp.int32, (groups, R), 0)
    level = spot % 4

    def joined(rows):
        return jnp.where(first, rows[0:groups], pltpu.roll(rows[groups:slabs], SLAB, 1))

    left_coef = from_left[SLAB + TERMS : SLAB + 2 * TERMS, :]
    right_coef = from_right[SLAB : SLAB + TERMS, :]
    above_coef = flipped(from_above[4 * slabs :, :])
    below_coef = flipped(from_below[4 * slabs :, :])
    for k in range(TERMS):
        rows = jnp.concatenate([coef[k * SLAB : (k + 1) * SLAB, :], jnp.zeros((SLAB, R - slabs), f32)], axis=1)
        own = joined(flipped(rows))
        half = pltpu.roll(own, SLAB, 1)
        left = jnp.where(first, left_coef[k : k + 1, :], half[groups - 1 : groups, :])
        left = jnp.where(group == 0, left, pltpu.roll(own, 1, 0))
        right = jnp.where(first, half[0:1, :], pltpu.roll(right_coef[k : k + 1, :], SLAB, 1))
        right = jnp.where(group == groups - 1, right, pltpu.roll(own, groups - 1, 0))
        up = jnp.where(
            spot < SLAB - 4,
            pltpu.roll(own, R - 4, 1),
            joined(pltpu.roll(above_coef, SLAB - 4 - 4 * k, 1)),
        )
        down = jnp.where(spot < 4, joined(pltpu.roll(below_coef, (R - 4 * k) % R, 1)), pltpu.roll(own, 4, 1))
        face[0, k] = 0.5 * (own + left)
        face[1, k] = 0.5 * (own + right)
        face[2, k] = 0.5 * (own + up)
        face[3, k] = 0.5 * (own + down)
        face[4, k] = 0.5 * (own + jnp.where(level < 3, pltpu.roll(own, R - 1, 1), 0.0))
        face[5, k] = 0.5 * (own + jnp.where(level > 0, pltpu.roll(own, 1, 1), 0.0))

    squares[...] = jnp.zeros_like(squares)
    lane = lax.broadcasted_iota(jnp.int32, (BLOCK, R), 1)
    inside = lane % SLAB
    depth = lane % 4

    def images(chunk, slot):
        for s in range(STEP):
            j = STEP * chunk + s
            weights = [[face[f, k, j : j + 1, :] for f in range(6)] for k in range(TERMS)]
            for start in range(0, R, BLOCK):
                rows = slice(start, start + BLOCK)
                v = turned[j, rows, :]
                up = pltpu.roll(above[rows, :], (SLAB - 4 - 4 * j) % R, 1)
                down = pltpu.roll(below[rows, :], (R - 4 * j) % R, 1)
                steps = (
                    v - strip(j - 1, rows),
                    v - strip(j + 1, rows),
                    v - jnp.where(inside < SLAB - 4, pltpu.roll(v, R - 4, 1), up),
                    v - jnp.where(inside < 4, down, pltpu.roll(v, 4, 1)),
                    v - jnp.where(depth < 3, pltpu.roll(v, R - 1, 1), 0.0),
                    v - jnp.where(depth > 0, pltpu.roll(v, 1, 1), 0.0),
                )
                summed_images = None
                for block in range(TERMS + 1):
                    if block == 0:
                        value = v
                    else:
                        k = block - 1
                        value = weights[k][0] * steps[0]
                        for weight, step in zip(weights[k][1:], steps[1:]):
                            value = value + weight * step
                        part = nominal_weights[k] * value
                        summed_images = part if summed_images is None else summed_images + part
                    high = value.astype(bf16)
                    rest = value - high.astype(f32)
                    squares[block, rows, :] += rest * rest
                    out = slice(block * R + start, block * R + start + BLOCK)
                    top[slot, out, s * R : (s + 1) * R] = high
                    bottom[slot, out, s * R : (s + 1) * R] = rest.astype(bf16)
                total[rows, :] = summed_images
            back = total[...].T
            nominal[j * SLAB : (j + 1) * SLAB, :] = back[0:SLAB]
            nominal[(j + groups) * SLAB : (j + groups + 1) * SLAB, :] = back[SLAB:]

    def grams(chunk, slot):
        for start in range(0, 2 * WIDTH, 256):
            rows = min(start + 256, WIDTH)
            if start + 256 <= WIDTH:
                right = top[slot, start : start + 256, :]
            elif start < WIDTH:
                right = jnp.concatenate([top[slot, start:WIDTH, :], bottom[slot, 0 : start + 256 - WIDTH, :]], axis=0)
            else:
                right = bottom[slot, start - WIDTH : start + 256 - WIDTH, :]
            value = lax.dot_general(
                top[slot, 0:rows, :], right, (((1,), (1,)), ((), ())), preferred_element_type=f32
            )
            if chunk == 0:
                product[0:rows, start : start + 256] = value
            else:
                product[0:rows, start : start + 256] += value

    chunks = groups // STEP
    for chunk in range(chunks):
        images(chunk, chunk % 2)
        if chunk > 0:
            grams(chunk - 1, (chunk - 1) % 2)
    grams(chunks - 1, (chunks - 1) % 2)

    r = lax.broadcasted_iota(jnp.int32, (R, R), 0)
    c = lax.broadcasted_iota(jnp.int32, (R, R), 1)

    def gram(a, b):
        high = product[a * R : (a + 1) * R, b * R : (b + 1) * R]
        one = product[a * R : (a + 1) * R, WIDTH + b * R : WIDTH + (b + 1) * R]
        two = product[b * R : (b + 1) * R, WIDTH + a * R : WIDTH + (a + 1) * R]
        if a != b:
            return high + one, two
        return high + one + jnp.where(r == c, jnp.sum(squares[a], axis=1, keepdims=True), 0.0), two

    def symmetric(a, b):
        one, two = gram(a, b)
        return one + two.T

    def diagonal(matrix):
        return jnp.sum(jnp.where(c == r, matrix, 0.0), axis=0, keepdims=True)

    base = symmetric(0, 0)
    for h, (even, full) in enumerate(halves):
        zero, one, two, three = [symmetric(*pair) for pair in even]
        tiles = [jnp.where(c >= r, base, zero), jnp.where(c >= r, one, two), jnp.where(c >= r, three, 0.0)]
        lines = []
        for line in (diagonal(zero), diagonal(two)):
            lines += [line, pltpu.roll(line, SLAB, 1)]
        for q, line in enumerate(lines):
            tiles[2] = jnp.where((r == R - 1 - q) & (c < SLAB), line, tiles[2])
        for pair in full:
            high, low = gram(*pair)
            tiles.append(high.T + low)

        def store(target, tiles=tiles):
            for q, tile in enumerate(tiles):
                target[q * R : (q + 1) * R, :] = tile

        pl.when(me[0] == h)(lambda: store(mine))
        pl.when(me[0] != h)(lambda: store(other))


def spread(value):
    return jnp.broadcast_to(value, (8, R))


def stacked(values, row8):
    out = values[-1]
    for i in range(len(values) - 2, -1, -1):
        out = jnp.where(row8 == i, values[i], out)
    return out


def panel_factor(rows, start):
    column = [spread(rows[:, start + l : start + l + 1]) for l in range(8)]
    a = [[spread(column[l][i : i + 1, :]) for l in range(i + 1)] for i in range(8)]
    inverse_pivot = [None] * 8
    lower = [[None] * 8 for _ in range(8)]
    for j in range(8):
        inverse_pivot[j] = 1.0 / a[j][j]
        for i in range(j + 1, 8):
            lower[i][j] = a[i][j] * inverse_pivot[j]
        for i in range(j + 1, 8):
            for l in range(j + 1, i + 1):
                a[i][l] = a[i][l] - lower[i][j] * a[l][j]
    turn = [[None] * 8 for _ in range(8)]
    for j in range(8):
        for i in range(j + 1, 8):
            value = lower[i][j]
            for l in range(j + 1, i):
                value = value + lower[i][l] * turn[l][j]
            turn[i][j] = -value
    return [a[j][j] for j in range(8)], inverse_pivot, turn


def factor_kernel(slot, inverse_t, inverse, *, cells):
    r = lax.broadcasted_iota(jnp.int32, (R, R), 0)
    c = lax.broadcasted_iota(jnp.int32, (R, R), 1)
    gram = jnp.where(c >= r, slot[...], slot[...].T) * (1.0 / cells)
    row8 = lax.broadcasted_iota(jnp.int32, (8, R), 0)
    lane8 = lax.broadcasted_iota(jnp.int32, (8, R), 1)
    panels = R // 8
    left = [gram[8 * i : 8 * i + 8, :] for i in range(panels)]
    right = [jnp.where(row8 + 8 * i == lane8, 1.0, 0.0).astype(f32) for i in range(panels)]
    for p in range(panels):
        start = 8 * p
        pivots, inverse_pivots, turn = panel_factor(left[p], start)
        ends = []
        for rows in (left[p], right[p]):
            out = rows
            for l in range(7):
                weight = jnp.where(row8 > l, turn[7][l], 0.0)
                for i in range(l + 1, 7):
                    weight = jnp.where(row8 == i, turn[i][l], weight)
                out = out + weight * spread(rows[l : l + 1, :])
            ends.append(out)
        inverse[start : start + 8, :] = ends[1] * stacked([1.0 / jnp.sqrt(pivot) for pivot in pivots], row8)
        if p == panels - 1:
            break
        scale = stacked(inverse_pivots, row8)
        solved = []
        for rows in ends:
            rows = rows * scale
            out = rows
            for i in range(1, 8):
                weight = jnp.where(row8 == 0, turn[i][0], 0.0)
                for l in range(1, i):
                    weight = jnp.where(row8 == l, turn[i][l], weight)
                out = out + weight * spread(rows[i : i + 1, :])
            solved.append(out)
        weights = [spread(left[p + 1][:, start + l : start + l + 1]) for l in range(8)]
        rest = left[p + 2 :]
        updates = []
        for out in solved:
            terms = [weights[l] * spread(out[l : l + 1, :]) for l in range(8)]
            while len(terms) > 1:
                terms = [terms[i] + terms[i + 1] for i in range(0, len(terms), 2)]
            updates.append(terms[0])
        left[p + 1] = left[p + 1] - updates[0]
        right[p + 1] = right[p + 1] - updates[1]
        if rest:
            columns = jnp.concatenate(rest, axis=0)[:, start : start + 8]
            update = jnp.dot(columns, jnp.concatenate(solved, axis=1), precision=HIGHEST, preferred_element_type=f32)
            for i in range(p + 2, panels):
                q = 8 * (i - p - 2)
                left[i] = left[i] - update[q : q + 8, :R]
                right[i] = right[i] - update[q : q + 8, R:]
    inverse_t[...] = inverse[...].T


def parts(value, count):
    out = []
    for _ in range(count):
        out.append(value.astype(bf16))
        value = value - out[-1].astype(f32)
    return out


def finish_kernel(
    me, mine, other, basis, nominal, inverse_t, ortho_hbm, nominal_hbm, reduced_hbm, residual_hbm,
    packed, ortho_out, nominal_out, reduced_out, residual_out, stage, sems, *, cells
):
    packed[pl.ds(pl.multiple_of(me[0] * HALF, R), HALF), :] = mine[...]
    packed[pl.ds(pl.multiple_of((1 - me[0]) * HALF, R), HALF), :] = other[...]
    high, middle, low = parts(inverse_t[...], 3)
    line = jnp.concatenate([high, middle], axis=1)
    square = jnp.concatenate([line, line], axis=0)
    last = jnp.concatenate([high, low], axis=0)

    def short(value):
        one, two = parts(value, 2)
        out = jnp.dot(jnp.concatenate([one, two], axis=1), square, preferred_element_type=f32)
        return out[:, :R] + out[:, R:]

    def product(value):
        one, two, three = parts(value, 3)
        out = jnp.dot(jnp.concatenate([one, two], axis=1), square, preferred_element_type=f32)
        end = jnp.dot(jnp.concatenate([three, one], axis=1), last, preferred_element_type=f32)
        return out[:, :R] + (out[:, R:] + end)

    copies = []

    def send(source, target):
        copies.append(pltpu.make_async_copy(source, target, sems.at[len(copies)]))
        copies[-1].start()

    step = 512
    for source, target, away in ((basis, ortho_out, ortho_hbm), (nominal, nominal_out, nominal_hbm)):
        for start in range(0, basis.shape[0], step):
            target[start : start + step, :] = short(source[start : start + step, :])
        send(target, away)

    r = lax.broadcasted_iota(jnp.int32, (R, R), 0)
    c = lax.broadcasted_iota(jnp.int32, (R, R), 1)
    scale = 1.0 / cells
    places = []
    for h, (even, full) in enumerate(halves):
        tiles = [packed[h * HALF + q * R : h * HALF + (q + 1) * R, :] for q in range(HALF_SLOTS)]
        turned = [tile.T for tile in tiles[:3]]
        lines = []
        for q in range(2):
            one = tiles[2][R - 1 - 2 * q : R - 2 * q, :]
            two = pltpu.roll(tiles[2][R - 2 - 2 * q : R - 1 - 2 * q, :], SLAB, 1)
            lines.append(jnp.where(c[0:1] < SLAB, one, two))
        matrices = [
            jnp.where(c < r, tiles[0], jnp.where(c == r, lines[0], turned[0])),
            jnp.where(c >= r, tiles[1], turned[1]),
            jnp.where(c < r, tiles[1], jnp.where(c == r, lines[1], turned[1])),
            jnp.where(c >= r, tiles[2], turned[2]),
        ] + tiles[3:]
        for (a, b), matrix in zip(even + full, matrices):
            at = len(places) * R
            stage[at : at + R, :] = matrix * scale
            places.append((reduced_out, b - 1) if a == 0 else (residual_out, operator_pairs.index((a - 1, b - 1))))
    moved = product(stage[...])
    for at in range(len(places)):
        stage[at * R : (at + 1) * R, :] = moved[at * R : (at + 1) * R, :].T
    moved = product(stage[...])
    for at, (target, index) in enumerate(places):
        target[index] = moved[at * R : (at + 1) * R, :]
    send(reduced_out, reduced_hbm)
    send(residual_out, residual_hbm)
    for copy in copies:
        copy.wait()


def summed(values, groups):
    count = lax.axis_size("gx")
    width = values.shape[1]
    parts = values.reshape(count, -1, width)
    shard = jnp.sum(lax.all_to_all(parts, "gx", 0, 0), axis=0)
    distance = len(groups)
    while distance < lax.axis_size("gy"):
        shard = shard + lax.ppermute(shard, "gy", [(i, i ^ distance) for i in range(lax.axis_size("gy"))])
        distance *= 2
    spread = jnp.broadcast_to(shard[None], (count,) + shard.shape)
    return lax.all_to_all(spread, "gx", 0, 0).reshape(values.shape)


def shards(raw_basis, coefficients, nominal_weights):
    nx, ny, nz, width = raw_basis.shape
    count_x, count_y = lax.axis_size("gx"), lax.axis_size("gy")
    cells = nx * ny * nz * count_x * count_y
    flat = raw_basis.reshape(-1, width)
    coef = jnp.transpose(coefficients, (0, 2, 3, 1)).reshape(-1, nx)
    vmem = pl.BlockSpec(memory_space=pltpu.VMEM)
    smem = pl.BlockSpec(memory_space=pltpu.SMEM)
    hbm = pl.BlockSpec(memory_space=pltpu.HBM)

    def array(*shape):
        return jax.ShapeDtypeStruct(shape, f32)

    me = jnp.stack([lax.axis_index("gy") % 2, lax.axis_index("gx") % 2]).astype(jnp.int32)
    small = pltpu.CompilerParams(vmem_limit_bytes=VMEM_LIMIT)
    x_rows, y_rows = SLAB + 2 * TERMS, 4 * nx + 4 * TERMS
    faces = pl.pallas_call(
        faces_kernel,
        out_shape=(array(x_rows, R), array(x_rows, R), array(y_rows, R), array(y_rows, R)),
        in_specs=[smem, hbm, hbm],
        out_specs=(vmem,) * 4,
        scratch_shapes=[
            pltpu.VMEM((SLAB, R), f32),
            pltpu.VMEM((SLAB, R), f32),
            pltpu.VMEM((nx, 8, R), f32),
            pltpu.VMEM((nx, 8, R), f32),
            pltpu.VMEM(coef.shape, f32),
            pltpu.SemaphoreType.DMA((5,)),
        ],
        compiler_params=small,
        name="faces",
    )(
        me,
        pltpu.with_memory_space_constraint(flat.reshape(nx, SLAB, width), pltpu.HBM),
        pltpu.with_memory_space_constraint(coef, pltpu.HBM),
    )

    def swaps(first, count):
        pairs = [(i, i + 1) for i in range(first, count - 1, 2)]
        return pairs + [(b, a) for a, b in pairs]

    halos = []
    for face, axis, first in zip(faces, ("gx", "gx", "gy", "gy"), (0, 1, 0, 1)):
        halos.append(lax.ppermute(face, axis, swaps(first, lax.axis_size(axis))))
    groups = nx // 2
    turned = pl.pallas_call(
        turn_kernel,
        out_shape=array(groups, R, R),
        in_specs=[vmem],
        out_specs=vmem,
        compiler_params=small,
        name="turn",
    )(flat)

    mine, other, raw_nominal = pl.pallas_call(
        images_kernel,
        out_shape=(array(HALF, R), array(HALF, R), array(nx * SLAB, R)),
        grid=(1,),
        in_specs=[smem, smem, vmem]
        + [pl.BlockSpec((SLAB, R), lambda i, at=at: (at, 0)) for at in (groups - 1, groups)]
        + [vmem] * 5,
        out_specs=(vmem,) * 3,
        scratch_shapes=[
            pltpu.VMEM((x_rows, R), f32),
            pltpu.VMEM((x_rows, R), f32),
            pltpu.VMEM((y_rows, R), f32),
            pltpu.VMEM((y_rows, R), f32),
            pltpu.VMEM((2, R, R), f32),
            pltpu.VMEM((R, 4 * nx), f32),
            pltpu.VMEM((R, 4 * nx), f32),
            pltpu.VMEM((6, TERMS, groups, R), f32),
            pltpu.VMEM((2, WIDTH, STEP * R), bf16),
            pltpu.VMEM((2, WIDTH, STEP * R), bf16),
            pltpu.VMEM((WIDTH, 2 * WIDTH), f32),
            pltpu.VMEM((TERMS + 1, R, R), f32),
            pltpu.VMEM((R, R), f32),
        ],
        compiler_params=small,
        name="images",
    )(me, nominal_weights, turned, flat, flat, coef, *halos)

    swap = [(i, i ^ 1) for i in range(count_y)]
    along_z = [list(range(core, count_y, 2)) for core in range(2)]
    mine = mine + lax.ppermute(other, "gy", swap)
    mine = summed(mine, along_z)
    other = lax.ppermute(mine, "gy", swap)

    def factor(*refs):
        factor_kernel(*refs, cells=cells)

    def finish(*refs):
        finish_kernel(*refs, cells=cells)

    inverse_t = pl.pallas_call(
        factor,
        out_shape=array(R, R),
        grid=(1,),
        in_specs=[pl.BlockSpec((R, R), lambda i: (0, 0))],
        out_specs=pl.BlockSpec((R, R), lambda i: (0, 0)),
        scratch_shapes=[pltpu.VMEM((R, R), f32)],
        compiler_params=small,
        name="factor",
    )(mine)
    ortho, nominal, reduced_ops, residual_grams = pl.pallas_call(
        finish,
        out_shape=(array(nx * SLAB, R), array(nx * SLAB, R), array(TERMS, R, R), array(len(operator_pairs), R, R)),
        in_specs=[smem] + [vmem] * 5,
        out_specs=(hbm,) * 4,
        scratch_shapes=[
            pltpu.VMEM((2 * HALF, R), f32),
            pltpu.VMEM((nx * SLAB, R), f32),
            pltpu.VMEM((nx * SLAB, R), f32),
            pltpu.VMEM((TERMS, R, R), f32),
            pltpu.VMEM((len(operator_pairs), R, R), f32),
            pltpu.VMEM(((TERMS + len(operator_pairs)) * R, R), f32),
            pltpu.SemaphoreType.DMA((4,)),
        ],
        compiler_params=small,
        name="finish",
    )(me, mine, other, flat, raw_nominal, inverse_t)
    shape = raw_basis.shape
    return (ortho.reshape(shape), nominal.reshape(shape), reduced_ops, residual_grams)


def solution(mesh):
    in_specs = (P("gx", "gy", None, None), P(None, "gx", "gy", None), P())
    out_specs = (P("gx", "gy", None, None), P("gx", "gy", None, None), P(), P())
    return jax.shard_map(shards, mesh=mesh, in_specs=in_specs, out_specs=out_specs, check_vma=False)
```
